512 devices in a mesh: seq: 8 (over x, z_hi), pos: 64 (over y, z_lo, core).
Axes of the slice: x: 4, y: 8, z: 8 (z_hi: 2, z_lo: 4; z = z_hi * 4 + z_lo), core: 2. Of those that a mesh axis runs over, the one named last changes fastest.
Arguments:
- skip_stream_input: bfloat16 [32, 512, 768], P('seq', 'pos'), may hold values from -6 to 6
- lateral_asking_vectors: bfloat16 [32, 512, 768], P('seq', 'pos'), may hold values from -30 to 30
- lateral_matched_vectors: bfloat16 [32, 512, 768], P('seq', 'pos'), may hold values from -6 to 6
- lateral_carried_vectors: bfloat16 [32, 512, 768], P('seq', 'pos'), may hold values from -6 to 6
- lateral_closing_linear: bfloat16 [768, 768], replicated, may hold values from -0.21875 to 0.21875
- upright_normalizer_multiplier: float32 [768], replicated, may hold values from 0.1 to 1.9
- upright_threefold_linear: bfloat16 [768, 2304], P(None, 'seq'), may hold values from -0.21875 to 0.21875
- upright_closing_linear: bfloat16 [768, 768], replicated, may hold values from -0.21875 to 0.21875
- regression_factors: float32 [12], replicated, may hold values from -768 to 768
- regression_offset: float32 [1], replicated, may hold values from -3 to 3
Outputs:
- alignment_output: bfloat16 [32, 512, 768], P('seq', 'pos')
- pairing_chances: float32 [512, 512], P('pos', 'seq')
The draws below stay inside these ranges and needn't reach their ends.
All inputs are finite; a program needn't handle non-finite values.
Results may differ from the reference program's by a relative error of at most 0.004.
Values may be sent and summed in bfloat16 or wider, within the bound.
A program may use at most 64 MiB of HBM per device.

```python
import jax
import jax.numpy as jnp
from jax import lax

EMBED_BREADTH = 768
FOCUS_GROUPS = 12
HEAD = 64
HOMOLOG_TOTAL = 32
COLUMN_SPAN = 512


def pair_fields(key):
    base_key = jax.random.fold_in(key, 101)
    key_query = jax.random.fold_in(base_key, 1)
    key_keys = jax.random.fold_in(base_key, 2)
    query_field = jnp.clip(jax.random.normal(key_query, (HOMOLOG_TOTAL, COLUMN_SPAN, EMBED_BREADTH), jnp.float32), -5.0, 5.0) * 1.2
    key_field = jnp.clip(jax.random.normal(key_keys, (HOMOLOG_TOTAL, COLUMN_SPAN, EMBED_BREADTH), jnp.float32), -5.0, 5.0) * 1.2
    return (query_field, key_field)


def draw_lateral_asking_vectors(key, part):
    return pair_fields(key)[0].astype(jnp.bfloat16)


def draw_lateral_matched_vectors(key, part):
    return pair_fields(key)[1].astype(jnp.bfloat16)


def block_levels(key, extent, split, smallest, top_value):
    level = 1.0
    for axis_at, blocks in split:
        steps = jax.random.uniform(jax.random.fold_in(jax.random.fold_in(key, 6), axis_at), (blocks,), jnp.float32, smallest / len(split), top_value / len(split))
        level = level * jnp.repeat(jnp.exp(steps), extent[axis_at] // blocks).reshape((-1,) + (1,) * (len(extent) - 1 - axis_at))
    return level


def scatter_about(rng, extent, width, bound, shards=(), dtype=jnp.bfloat16):
    result = width * jax.random.normal(rng, extent, jnp.float32)
    if shards:
        result = result * block_levels(rng, extent, shards, -0.22, 0.18)
    return jnp.clip(result, -bound, bound).astype(dtype)


def setup_inputs(seed: int = 0) -> dict:
    arg_keys = jax.random.split(jax.random.key(seed), 11)
    skip_stream_input = scatter_about(arg_keys[0], (HOMOLOG_TOTAL, COLUMN_SPAN, EMBED_BREADTH), 1.0, 6.0, ((0, 8), (1, 64)))
    lateral_asking_vectors = draw_lateral_asking_vectors(jax.random.fold_in(arg_keys[10], 71), 0)
    lateral_matched_vectors = draw_lateral_matched_vectors(jax.random.fold_in(arg_keys[10], 71), 0)
    lateral_carried_vectors = scatter_about(arg_keys[3], (HOMOLOG_TOTAL, COLUMN_SPAN, EMBED_BREADTH), 1.0, 6.0, ((0, 8), (1, 64)))
    lateral_closing_linear = scatter_about(arg_keys[4], (EMBED_BREADTH, EMBED_BREADTH), EMBED_BREADTH ** -0.5, 0.21875)
    upright_normalizer_multiplier = jnp.clip(1.0 + 0.18 * jax.random.normal(arg_keys[5], (EMBED_BREADTH,), jnp.float32), 0.1, 1.9)
    upright_threefold_linear = scatter_about(arg_keys[6], (EMBED_BREADTH, 3 * EMBED_BREADTH), EMBED_BREADTH ** -0.5, 0.21875, ((1, 8),))
    upright_closing_linear = scatter_about(arg_keys[7], (EMBED_BREADTH, EMBED_BREADTH), EMBED_BREADTH ** -0.5, 0.21875)
    regression_factors = scatter_about(arg_keys[8], (FOCUS_GROUPS,), (COLUMN_SPAN // 4), 768.0, (), jnp.float32)
    regression_offset = scatter_about(arg_keys[9], (1,), 1.0, 3.0, (), jnp.float32)
    return {"skip_stream_input": skip_stream_input, "lateral_asking_vectors": lateral_asking_vectors, "lateral_matched_vectors": lateral_matched_vectors, "lateral_carried_vectors": lateral_carried_vectors, "lateral_closing_linear": lateral_closing_linear, "upright_normalizer_multiplier": upright_normalizer_multiplier, "upright_threefold_linear": upright_threefold_linear, "upright_closing_linear": upright_closing_linear, "regression_factors": regression_factors, "regression_offset": regression_offset}


def layer_norm(values, scaling):
    average = lax.optimization_barrier(jnp.mean(values, axis=-1, keepdims=True))
    centered = values - average
    spread = lax.optimization_barrier(jnp.mean(centered * centered, axis=-1, keepdims=True))
    return centered * lax.rsqrt(spread + 1e-05) * scaling

def softmax_last(scores):
    row_peak = lax.optimization_barrier(jnp.max(scores, axis=-1, keepdims=True))
    exponent = jnp.exp(scores - row_peak)
    return exponent / lax.optimization_barrier(jnp.sum(exponent, axis=-1, keepdims=True))

def softmax_plain(scores):
    exponent = jnp.exp(scores)
    return exponent / lax.optimization_barrier(jnp.sum(exponent, axis=-1, keepdims=True))

def reference(skip_stream_input, lateral_asking_vectors, lateral_matched_vectors, lateral_carried_vectors, lateral_closing_linear, upright_normalizer_multiplier, upright_threefold_linear, upright_closing_linear, regression_factors, regression_offset):
    upper_limit = lax.Precision.HIGHEST
    queries = lateral_asking_vectors.astype(jnp.float32).reshape(HOMOLOG_TOTAL, COLUMN_SPAN, FOCUS_GROUPS, HEAD)
    key_rows = lateral_matched_vectors.astype(jnp.float32).reshape(HOMOLOG_TOTAL, COLUMN_SPAN, FOCUS_GROUPS, HEAD)
    factor = 1.0 / (jnp.sqrt(jnp.float32(HEAD)) * jnp.sqrt(jnp.float32(HOMOLOG_TOTAL)))
    logits = jnp.einsum('rihd,rjhd->hij', queries, key_rows, precision=upper_limit) * factor
    affinity_shares = softmax_last(logits).astype(jnp.bfloat16)
    value_rows = lateral_carried_vectors.astype(jnp.float32).reshape(HOMOLOG_TOTAL, COLUMN_SPAN, FOCUS_GROUPS, HEAD)
    mixture = jnp.einsum('hij,rjhd->rihd', affinity_shares.astype(jnp.float32), value_rows, precision=upper_limit)
    horizontal_mixed_result = mixture.astype(jnp.bfloat16).reshape(HOMOLOG_TOTAL * COLUMN_SPAN, EMBED_BREADTH)
    residue_embedding = skip_stream_input.reshape(HOMOLOG_TOTAL * COLUMN_SPAN, EMBED_BREADTH).astype(jnp.float32) + jnp.dot(horizontal_mixed_result, lateral_closing_linear, preferred_element_type=jnp.float32)
    normed = layer_norm(residue_embedding, upright_normalizer_multiplier).astype(jnp.bfloat16)
    projected = jnp.dot(normed, upright_threefold_linear, preferred_element_type=jnp.float32).astype(jnp.bfloat16)
    projected = projected.reshape(HOMOLOG_TOTAL, COLUMN_SPAN, 3, FOCUS_GROUPS, HEAD).astype(jnp.float32)
    col_query = projected[:, :, 0]
    col_key = projected[:, :, 1]
    col_value = projected[:, :, 2]
    col_scores = jnp.einsum('sphd,tphd->phst', col_query, col_key, precision=upper_limit) * (1.0 / jnp.sqrt(jnp.float32(HEAD)))
    col_weights = softmax_plain(col_scores).astype(jnp.bfloat16)
    column_mixing = jnp.einsum('phst,tphd->sphd', col_weights.astype(jnp.float32), col_value, precision=upper_limit)
    column_mixing = column_mixing.astype(jnp.bfloat16).reshape(HOMOLOG_TOTAL * COLUMN_SPAN, EMBED_BREADTH)
    alignment_output = (residue_embedding + jnp.dot(column_mixing, upright_closing_linear, preferred_element_type=jnp.float32)).astype(jnp.bfloat16)
    affinity_grids = affinity_shares.astype(jnp.float32)
    couple_amount = lax.optimization_barrier(jnp.sum(affinity_grids, axis=1)) + lax.optimization_barrier(jnp.sum(affinity_grids, axis=2))
    focus_group_amount = lax.optimization_barrier(jnp.sum(couple_amount, axis=1))
    combined_groups = jnp.einsum('f,feg->eg', regression_factors, affinity_grids, precision=upper_limit)
    product_adjuster = jnp.einsum('q,qz,qd->zd', regression_factors / focus_group_amount, couple_amount, couple_amount, precision=upper_limit)
    pairing_chances = jax.nn.sigmoid(combined_groups + combined_groups.T - product_adjuster + regression_offset[0])
    return (alignment_output.reshape(HOMOLOG_TOTAL, COLUMN_SPAN, EMBED_BREADTH), pairing_chances)
```

```python
import math

import jax
import jax.numpy as jnp
from jax import lax
from jax.experimental import pallas as pl
from jax.experimental.pallas import tpu as pltpu
from jax.sharding import PartitionSpec as P

MESH = pl.DeviceIdType.MESH
HI = lax.Precision.HIGHEST
F32 = jnp.float32
BF16 = jnp.bfloat16
NT = (((1,), (1,)), ((), ()))
CHUNKS = 2


def body(
    skip_hbm, q_hbm, k_hbm, v_hbm, wc_hbm, gain_ref, w3_hbm, wo_hbm, factor_ref, offset_ref,
    out_ref, pair_ref,
    qg, kg, vg, wb, wc, wo, sk,
    part, rs, wm, wg, wf, nf, nm, ng, cm, cg, hid, proj,
    ptl, ptz, pty, pts, mloc, mrow, mcol, stage,
    lsem, ssem, rq, rqs, rk, rva, rvs, rvr, rwx, rww, rrs, rwg, rng, rcg, rpz, rpy, rps, rm1, rm2,
):
    s = lax.axis_index("seq")
    p = lax.axis_index("pos")
    x, zh = s // 2, s % 2
    y, zc = p // 8, p % 8
    zl, c = zc // 2, zc % 2
    sib = y * 8 + zl * 2 + (1 - c)
    partner = x * 2 + (1 - zh)

    def local(src, dst, index):
        copy = pltpu.make_async_copy(src, dst, lsem.at[index])
        copy.start()
        return copy

    def send(src, dst, send_sem, recv_sem, seq, pos):
        pltpu.make_async_remote_copy(
            src_ref=src, dst_ref=dst, send_sem=send_sem, recv_sem=recv_sem,
            device_id=(seq, pos), device_id_type=MESH,
        ).start()

    def wait(ref, sem):
        pltpu.make_async_copy(ref, ref, sem).wait()

    loads = [
        local(q_hbm, qg.at[zc], 0),
        local(k_hbm, kg.at[y], 1),
        local(v_hbm, vg.at[c, y, zl], 2),
        local(w3_hbm, wb.at[s], 3),
        local(wc_hbm, wc, 4),
        local(wo_hbm, wo, 5),
        local(skip_hbm, sk, 6),
    ]

    barrier = pltpu.get_barrier_semaphore()
    plane = s * 8 + zc

    def greet(d, carry):
        o = (plane + d) % 64
        pl.semaphore_signal(barrier, inc=1, device_id=(o // 8, y * 8 + o % 8), device_id_type=MESH)
        return carry

    lax.fori_loop(1, 64, greet, 0)
    for d in range(1, 8):
        pl.semaphore_signal(
            barrier, inc=1, device_id=(s, ((y + d) % 8) * 8 + zc), device_id_type=MESH
        )
    pl.semaphore_wait(barrier, 70)

    y_order = (1, 7, 2, 6, 3, 5, 4)
    send(q_hbm, qg.at[zc], ssem.at[0], rqs.at[zl], s, sib)
    for d in (1, 3, 2):
        send(q_hbm, qg.at[zc], ssem.at[1], rq.at[zl], s, y * 8 + ((zl + d) % 4) * 2 + c)
    for d in y_order:
        send(k_hbm, kg.at[y], ssem.at[2], rk, s, ((y + d) % 8) * 8 + zc)
    for d in (1, 3, 2):
        send(v_hbm, vg.at[c, y, zl], ssem.at[3], rva, s, y * 8 + ((zl + d) % 4) * 2 + c)

    rows = 384 // CHUNKS

    def w_rows(ch):
        return pl.ds(pl.multiple_of(c * 384 + ch * rows, rows), rows)

    def w_own(ch):
        for d in (1, 3, 2):
            send(
                w3_hbm.at[w_rows(ch), :], wb.at[s, w_rows(ch), :], ssem.at[4 + ch],
                rwx.at[ch, (4 - d) % 4], ((x + d) % 4) * 2 + zh, p,
            )

    def w_over(ch):
        send(
            w3_hbm.at[w_rows(ch), :], wb.at[s, w_rows(ch), :], ssem.at[6 + ch],
            rwx.at[ch, 4], partner, p,
        )

    def w_relay(ch):
        wait(wb.at[partner, w_rows(ch), :], rwx.at[ch, 4])
        for d in (1, 3, 2):
            send(
                wb.at[partner, w_rows(ch), :], wb.at[partner, w_rows(ch), :], ssem.at[8 + ch],
                rwx.at[ch, 4 + (4 - d) % 4], ((x + d) % 4) * 2 + zh, p,
            )
        send(
            wb.at[partner, w_rows(ch), :], wb.at[partner, w_rows(ch), :], ssem.at[10],
            rww, s, sib,
        )

    def w_sibling(ch, far):
        for d in (1, 3, 2):
            shard = ((x + d) % 4) * 2 + (partner % 2 if far else zh)
            wait(wb.at[shard, w_rows(ch), :], rwx.at[ch, (4 if far else 0) + d])
            send(
                wb.at[shard, w_rows(ch), :], wb.at[shard, w_rows(ch), :], ssem.at[10],
                rww, s, sib,
            )

    for ch in range(CHUNKS):
        w_own(ch)
    w_over(0)

    part[:, 6:8, :] = jnp.zeros((64, 2, 128), F32)

    for d in (1, 3, 2):
        other = (zl + d) % 4
        wait(qg.at[0], rq.at[other])
        send(
            qg.at[other * 2 + c], qg.at[other * 2 + c], ssem.at[0], rqs.at[other], s, sib
        )
    loads[0].wait()
    loads[1].wait()
    for other in range(4):
        wait(qg.at[0], rqs.at[other])
    wait(kg.at[0:7], rk)

    lane64 = lax.broadcasted_iota(jnp.int32, (64, 128), 1) < 64
    zero64 = jnp.zeros((64, 128), BF16)
    for k in range(6):
        left = jnp.concatenate([qg[:, r, k].reshape(64, 128) for r in range(4)], axis=1)
        keys = [kg[:, r, k].reshape(64, 128) for r in range(4)]
        low = jnp.concatenate([jnp.where(lane64, b, zero64) for b in keys], axis=1)
        high = jnp.concatenate([jnp.where(lane64, zero64, b) for b in keys], axis=1)
        tile = lax.dot_general(
            left, jnp.concatenate([low, high], axis=0), NT, preferred_element_type=F32
        )
        part[:, k, :] = tile

    own = pltpu.make_async_copy(part.at[zc * 8 + s], rs.at[plane], lsem.at[7])
    own.start()

    def scatter(d, carry):
        o = (plane + d) % 64
        so, zo = o // 8, o % 8
        send(part.at[zo * 8 + so], rs.at[plane], ssem.at[11], rrs, so, y * 8 + zo)
        return carry

    lax.fori_loop(1, 64, scatter, 0)

    up, down = ((y + 1) % 8) * 8 + zc, ((y + 7) % 8) * 8 + zc

    def v_send(block, step, halves):
        if halves:
            send(
                vg.at[c, block[0], 0:2], vg.at[c, block[0], 0:2], ssem.at[12], rvr.at[0, step], s, up
            )
            send(
                vg.at[c, block[1], 2:4], vg.at[c, block[1], 2:4], ssem.at[12], rvr.at[1, step], s, down
            )
            return
        send(vg.at[c, block[0]], vg.at[c, block[0]], ssem.at[13], rvr.at[0, step], s, up)
        send(vg.at[c, block[1]], vg.at[c, block[1]], ssem.at[13], rvr.at[1, step], s, down)

    def v_sib(block):
        send(vg.at[c, block], vg.at[c, block], ssem.at[14], rvs, s, sib)

    loads[2].wait()
    wait(vg.at[0, 0, 0:3], rva)
    v_send((y, y), 0, False)
    v_sib(y)

    def v_step(step):
        below, above = (y + 8 - step) % 8, (y + step) % 8
        wait(vg.at[0, 0], rvr.at[0, step - 1])
        wait(vg.at[0, 0], rvr.at[1, step - 1])
        v_send((below, above), step, step == 3)
        v_sib(below)
        v_sib(above)

    v_step(1)

    own.wait()
    wait(rs.at[0:63], rrs)
    logits = rs[0:8]
    for so in range(1, 8):
        logits = logits + rs[so * 8 : so * 8 + 8]
    logits = logits * (1.0 / (math.sqrt(64) * math.sqrt(32)))
    lane8 = lax.broadcasted_iota(jnp.int32, (8, 128), 1)
    lower = lane8 < 64
    peak = jnp.max(logits, axis=0)
    neg = jnp.full((8, 128), -jnp.inf, F32)
    peak_low = jnp.max(jnp.where(lower, peak, neg), axis=1, keepdims=True)
    peak_high = jnp.max(jnp.where(lower, neg, peak), axis=1, keepdims=True)
    exponent = jnp.exp(logits - jnp.where(lower, peak_low, peak_high)[None])
    total = jnp.sum(exponent, axis=0)
    zero8 = jnp.zeros((8, 128), F32)
    total_low = jnp.sum(jnp.where(lower, total, zero8), axis=1, keepdims=True)
    total_high = jnp.sum(jnp.where(lower, zero8, total), axis=1, keepdims=True)
    weights = exponent / jnp.where(lower, total_low, total_high)[None]
    for z in range(4):
        even, odd = weights[2 * z], weights[2 * z + 1]
        wm[z] = jnp.where(lower, even, pltpu.roll(odd, 64, 1)).astype(BF16)
        wm[4 + z] = jnp.where(lower, pltpu.roll(even, 64, 1), odd).astype(BF16)

    seq_order = (7, 1, 2, 6, 3, 5, 4)
    keep = pltpu.make_async_copy(wm, wg.at[s], lsem.at[8])
    keep.start()
    for d in seq_order:
        send(wm, wg.at[s], ssem.at[15], rwg, (s + d) % 8, p)
    for ch in range(1, CHUNKS):
        w_over(ch)

    for step in (2, 3):
        v_step(step)
    w_relay(0)

    keep.wait()
    wait(wg.at[0:7], rwg)
    wf[...] = wg[...].astype(F32)

    sums = wf[0]
    for i in range(1, 8):
        sums = sums + wf[i]
    base = c * 64 + y * 8
    for hh in range(2):
        placed = zero8
        for i in range(8):
            block = wf[i, hh * 4] + wf[i, hh * 4 + 1] + wf[i, hh * 4 + 2] + wf[i, hh * 4 + 3]
            placed = placed + jnp.where(
                lane8 == base + i, jnp.sum(block, axis=1, keepdims=True), zero8
            )
        for z in range(4):
            here = (zl == z).astype(F32)
            ptl[hh * 4 + z] = sums[hh * 4 + z] + here * placed
    ptz[zc] = ptl[s]
    for d in range(1, 8):
        send(ptl.at[s], ptz.at[zc], ssem.at[16], rpz, s, y * 8 + (zc + d) % 8)

    for z in range(4):
        acc = zero8
        for k in range(6):
            for hh in range(2):
                acc = acc + factor_ref[2 * k + hh] * wf[:, hh * 4 + z, k, :]
        mloc[z] = acc

    @pl.when(y == s)
    def _():
        for d in y_order:
            send(mloc, mrow, ssem.at[17], rm1, s, ((y + d) % 8) * 8 + zc)

    for step in (3,):
        wait(vg.at[0, 0, 0:2], rvr.at[0, step])
        wait(vg.at[0, 0, 2:4], rvr.at[1, step])
    opposite = (y + 4) % 8
    v_sib(opposite)
    wait(vg.at[0], rvs)

    lower16 = lax.broadcasted_iota(jnp.int32, (8, 512), 1) % 128 < 64
    mixed = []
    for k in range(6):
        left = jnp.concatenate(
            [
                jnp.concatenate([wf[:, hh * 4 + z, k, :] for z in range(4)], axis=1)
                for hh in range(2)
            ],
            axis=0,
        ).astype(BF16)
        right = jnp.concatenate(
            [
                jnp.concatenate(
                    [vg[:, :, z, r, k].reshape(128, 128) for z in range(4)], axis=0
                )
                for r in range(4)
            ],
            axis=1,
        )
        both = jnp.dot(left, right, preferred_element_type=F32)
        mixed.append(jnp.where(lower16, both[0:8], both[8:16]))
    row_out = jnp.concatenate(
        [
            jnp.concatenate([mixed[k][:, r * 128 : r * 128 + 128] for k in range(6)], axis=1)
            for r in range(4)
        ],
        axis=0,
    ).astype(BF16)
    loads[4].wait()
    loads[6].wait()
    skip = jnp.concatenate(
        [
            jnp.concatenate([sk[r, k].astype(F32) for k in range(6)], axis=1)
            for r in range(4)
        ],
        axis=0,
    )
    hidden = skip + jnp.dot(row_out, wc[...], preferred_element_type=F32)
    hid[...] = hidden
    average = jnp.mean(hidden, axis=1, keepdims=True)
    centered = hidden - average
    spread = jnp.mean(centered * centered, axis=1, keepdims=True)
    normed = centered * lax.rsqrt(spread + 1e-05) * gain_ref[...]
    for r in range(4):
        for k in range(6):
            nf[:, r * 6 + k, :] = normed[r * 8 : r * 8 + 8, k * 128 : k * 128 + 128]
    nm[...] = nf[...].astype(BF16)
    keep = pltpu.make_async_copy(nm.at[s], ng.at[s], lsem.at[9])
    keep.start()
    for d in seq_order:
        send(nm.at[(s + d) % 8], ng.at[s], ssem.at[18], rng, (s + d) % 8, p)

    for ch in range(1, CHUNKS):
        w_relay(ch)
    for ch in range(CHUNKS):
        w_sibling(ch, False)

    wait(ptz.at[0:7], rpz)
    acc = ptz[0]
    for z in range(1, 8):
        acc = acc + ptz[z]
    stage[0] = acc
    pty[y] = acc
    for d in y_order:
        send(stage.at[0], pty.at[y], ssem.at[19], rpy, s, ((y + d) % 8) * 8 + zc)
    for ch in range(CHUNKS):
        w_sibling(ch, True)
    loads[3].wait()
    wait(wb.at[0:7, 0:384, :], rww)

    def unpack(ref):
        nf[...] = ref[...].astype(F32)
        return jnp.concatenate(
            [
                jnp.concatenate([nf[:, r * 6 + k, :] for k in range(6)], axis=1)
                for r in range(4)
            ],
            axis=0,
        ).astype(BF16)

    keep.wait()
    wait(ng.at[0:7], rng)
    cells = unpack(ng)
    for so in range(8):
        proj[:, so * 288 : so * 288 + 288] = jnp.dot(
            cells, wb[so], preferred_element_type=F32
        )
    lane32 = lax.broadcasted_iota(jnp.int32, (32, 128), 1) < 64
    zero32 = jnp.zeros((32, 128), BF16)
    outs = []
    for k in range(6):
        cq = proj[:, k * 128 : k * 128 + 128].astype(BF16)
        ck = proj[:, 768 + k * 128 : 768 + k * 128 + 128].astype(BF16)
        cv = proj[:, 1536 + k * 128 : 1536 + k * 128 + 128].astype(BF16)
        left = jnp.concatenate(
            [jnp.where(lane32, cq, zero32), jnp.where(lane32, zero32, cq)], axis=0
        )
        score = lax.dot_general(left, ck, NT, preferred_element_type=F32) * (1.0 / math.sqrt(64))
        exponent = jnp.exp(score)
        share = (exponent / jnp.sum(exponent, axis=1, keepdims=True)).astype(BF16)
        both = jnp.dot(share, cv, preferred_element_type=F32)
        outs.append(jnp.where(lane32, both[0:32], both[32:64]))
    for r in range(4):
        for k in range(6):
            nf[:, r * 6 + k, :] = outs[k][r * 8 : r * 8 + 8]
    cm[...] = nf[...].astype(BF16)
    keep = pltpu.make_async_copy(cm.at[s], cg.at[s], lsem.at[10])
    keep.start()
    for d in seq_order:
        send(cm.at[(s + d) % 8], cg.at[s], ssem.at[20], rcg, (s + d) % 8, p)

    wait(pty.at[0:7], rpy)
    acc = pty[0]
    for o in range(1, 8):
        acc = acc + pty[o]
    stage[1] = acc
    pts[s] = acc
    for d in seq_order:
        send(stage.at[1], pts.at[s], ssem.at[21], rps, (s + d) % 8, p)

    @pl.when(y == s)
    def _():
        mrow[...] = mloc[...]

    @pl.when(y != s)
    def _():
        wait(mrow, rm1)

    mcol[zc] = mrow[zl]
    for d in range(1, 8):
        o = (zc + d) % 8
        send(mrow.at[o // 2], mcol.at[zc], ssem.at[22], rm2, s, y * 8 + o)

    loads[5].wait()
    keep.wait()
    wait(cg.at[0:7], rcg)
    cells = unpack(cg)
    closing = hid[...] + jnp.dot(cells, wo[...], preferred_element_type=F32)
    for r in range(4):
        for k in range(6):
            out_ref[r, k] = closing[r * 8 : r * 8 + 8, k * 128 : k * 128 + 128].astype(BF16)

    wait(pts.at[0:7], rps)
    wait(mcol.at[0:7], rm2)
    row8 = lax.broadcasted_iota(jnp.int32, (8, 128), 0)
    scaled, cols = [], []
    for hh in range(2):
        whole = pts[hh * 4] + pts[hh * 4 + 1] + pts[hh * 4 + 2] + pts[hh * 4 + 3]
        head_total = jnp.sum(whole, axis=1, keepdims=True)
        factor = zero8
        for k in range(6):
            factor = jnp.where(row8 == k, factor_ref[2 * k + hh], factor)
        scaled.append(factor / head_total * pts[hh * 4 + zl])
    block = jnp.zeros((24, 64), F32)
    lane_at = lax.broadcasted_iota(jnp.int32, (128, 64), 0)
    col_at = lax.broadcasted_iota(jnp.int32, (128, 64), 1)
    wanted = ((col_at // 8) % 2) * 64 + s * 8 + col_at % 8
    for z in range(4):
        pick = jnp.where((lane_at == wanted) & (col_at // 16 == z), 1.0, 0.0).astype(F32)
        block = block + jnp.dot(
            jnp.concatenate([pts[z], pts[4 + z], mloc[z]], axis=0), pick,
            precision=HI, preferred_element_type=F32,
        )
    mine = jnp.where(lane8 == base + row8, 1.0, 0.0).astype(F32)
    rows_here = lax.dot_general(
        mine, jnp.concatenate(scaled, axis=0), NT, precision=HI, preferred_element_type=F32
    )
    product = jnp.dot(rows_here, block[0:16], precision=HI, preferred_element_type=F32)
    mirrored = lax.dot_general(
        mine, mcol[...].reshape(64, 128), NT, precision=HI, preferred_element_type=F32
    )
    pair_ref[...] = jax.nn.sigmoid(block[16:24] + mirrored - product + offset_ref[0])

    wait(qg.at[0:4], ssem.at[0])
    wait(qg.at[0:3], ssem.at[1])
    wait(kg.at[0:7], ssem.at[2])
    wait(vg.at[0, 0, 0:3], ssem.at[3])
    for ch in range(CHUNKS):
        wait(wb.at[0:3, 0:rows, :], ssem.at[4 + ch])
        wait(wb.at[0, 0:rows, :], ssem.at[6 + ch])
        wait(wb.at[0:3, 0:rows, :], ssem.at[8 + ch])
    wait(wb.at[0:7, 0:384, :], ssem.at[10])
    wait(rs.at[0:63], ssem.at[11])
    wait(vg.at[0, 0], ssem.at[12])
    wait(vg.at[0, 0:6], ssem.at[13])
    wait(vg.at[0], ssem.at[14])
    wait(wg.at[0:7], ssem.at[15])
    wait(ptz.at[0:7], ssem.at[16])

    @pl.when(y == s)
    def _():
        wait(rs.at[0:28], ssem.at[17])

    wait(ng.at[0:7], ssem.at[18])
    wait(pty.at[0:7], ssem.at[19])
    wait(cg.at[0:7], ssem.at[20])
    wait(pts.at[0:7], ssem.at[21])
    wait(mcol.at[0:7], ssem.at[22])


def per_device(
    skip_stream_input,
    lateral_asking_vectors,
    lateral_matched_vectors,
    lateral_carried_vectors,
    lateral_closing_linear,
    upright_normalizer_multiplier,
    upright_threefold_linear,
    upright_closing_linear,
    regression_factors,
    regression_offset,
):
    def tiles(array):
        return array.reshape(4, 8, 6, 128).transpose(0, 2, 1, 3)

    def vmem(*shape, dtype=BF16):
        return pltpu.VMEM(shape, dtype)

    def dma(*shape):
        return pltpu.SemaphoreType.DMA(shape)

    anywhere = pl.BlockSpec(memory_space=pl.ANY)
    in_vmem = pl.BlockSpec(memory_space=pltpu.VMEM)
    in_smem = pl.BlockSpec(memory_space=pltpu.SMEM)
    one = pltpu.SemaphoreType.DMA
    aligned, pairs = pl.pallas_call(
        body,
        out_shape=(
            jax.ShapeDtypeStruct((4, 6, 8, 128), BF16),
            jax.ShapeDtypeStruct((8, 64), F32),
        ),
        in_specs=[
            anywhere, anywhere, anywhere, anywhere, anywhere, in_vmem, anywhere, anywhere,
            in_smem, in_smem,
        ],
        out_specs=(in_vmem, in_vmem),
        scratch_shapes=[
            vmem(8, 4, 6, 8, 128),
            vmem(8, 4, 6, 8, 128),
            vmem(2, 8, 4, 4, 6, 8, 128),
            vmem(8, 768, 288),
            vmem(768, 768),
            vmem(768, 768),
            vmem(4, 6, 8, 128),
            vmem(64, 8, 128, dtype=F32),
            vmem(64, 8, 128, dtype=F32),
            vmem(8, 8, 128),
            vmem(8, 8, 8, 128),
            vmem(8, 8, 8, 128, dtype=F32),
            vmem(8, 24, 128, dtype=F32),
            vmem(8, 24, 128),
            vmem(8, 24, 128),
            vmem(8, 24, 128),
            vmem(8, 24, 128),
            vmem(32, 768, dtype=F32),
            vmem(32, 2304, dtype=F32),
            vmem(8, 8, 128, dtype=F32),
            vmem(8, 8, 128, dtype=F32),
            vmem(8, 8, 128, dtype=F32),
            vmem(8, 8, 128, dtype=F32),
            vmem(4, 8, 128, dtype=F32),
            vmem(4, 8, 128, dtype=F32),
            vmem(8, 8, 128, dtype=F32),
            vmem(2, 8, 128, dtype=F32),
            dma(11),
            dma(23),
            dma(4),
            dma(4),
            one,
            one,
            one,
            dma(2, 4),
            dma(CHUNKS, 8),
            one,
            one,
            one,
            one,
            one,
            one,
            one,
            one,
            one,
            one,
        ],
        compiler_params=pltpu.CompilerParams(
            collective_id=0, has_side_effects=True, vmem_limit_bytes=48 << 20
        ),
        name="axial_layer",
    )(
        tiles(skip_stream_input),
        tiles(lateral_asking_vectors),
        tiles(lateral_matched_vectors),
        tiles(lateral_carried_vectors),
        lateral_closing_linear,
        upright_normalizer_multiplier.reshape(1, 768),
        upright_threefold_linear,
        upright_closing_linear,
        regression_factors,
        regression_offset,
    )
    return aligned.transpose(0, 2, 1, 3).reshape(4, 8, 768), pairs


def solution(mesh):
    placed = (
        P("seq", "pos", None),
        P("seq", "pos", None),
        P("seq", "pos", None),
        P("seq", "pos", None),
        P(),
        P(),
        P(None, "seq"),
        P(),
        P(),
        P(),
    )
    return jax.shard_map(
        per_device,
        mesh=mesh,
        in_specs=placed,
        out_specs=(P("seq", "pos", None), P("pos", "seq")),
        check_vma=False,
    )
```

```python
import math

import jax
import jax.numpy as jnp
from jax import lax
from jax.experimental import pallas as pl
from jax.experimental.pallas import tpu as pltpu
from jax.sharding import PartitionSpec as P

MESH = pl.DeviceIdType.MESH
HI = lax.Precision.HIGHEST
F32 = jnp.float32
BF16 = jnp.bfloat16
NT = (((1,), (1,)), ((), ()))
CHUNKS = 2
W_AT, W_ROWS = (0, 80), (80, 64)


def body(
    skip_hbm, q_hbm, k_hbm, v_hbm, wc_hbm, gain_hbm, w3_hbm, wo_hbm, factor_hbm, offset_ref,
    out_ref, pair_ref,
    qg, kg, vg, wb, wc, wo, sk,
    part, rs, wm, wg, wf, nf, nm, ng, cm, cg, hid, proj, gain, factor_ref,
    ptl, ptz, pty, pts, mloc, mrow, mcol, stage,
    lsem, ssem, rq, rqs, rk, rva, rvs, rvr, rwx, rww, rrs, rwg, rng, rcg, rpz, rpy, rps, rm1, rm2,
):
    s = lax.axis_index("seq")
    p = lax.axis_index("pos")
    x, zh = s // 2, s % 2
    y, zc = p // 8, p % 8
    zl, c = zc // 2, zc % 2
    sib = y * 8 + zl * 2 + (1 - c)
    partner = x * 2 + (1 - zh)

    def local(src, dst, index):
        copy = pltpu.make_async_copy(src, dst, lsem.at[index])
        copy.start()
        return copy

    def send(src, dst, send_sem, recv_sem, seq, pos):
        pltpu.make_async_remote_copy(
            src_ref=src, dst_ref=dst, send_sem=send_sem, recv_sem=recv_sem,
            device_id=(seq, pos), device_id_type=MESH,
        ).start()

    def wait(ref, sem):
        pltpu.make_async_copy(ref, ref, sem).wait()

    loads = [
        local(q_hbm, qg.at[zc], 0),
        local(k_hbm, kg.at[y], 1),
        local(v_hbm, vg.at[c, y, zl], 2),
        local(w3_hbm, wb.at[pl.ds(pl.multiple_of(s * 288, 16), 288), :], 3),
        local(wc_hbm, wc, 4),
        local(wo_hbm, wo, 5),
        local(skip_hbm, sk, 6),
        local(gain_hbm, gain, 11),
        local(factor_hbm, factor_ref, 12),
    ]

    barrier = pltpu.get_barrier_semaphore()
    plane = s * 8 + zc

    for d in range(1, 64):
        pl.semaphore_signal(
            barrier, inc=1, device_id=((s + d // 8) % 8, y * 8 + (zc + d % 8) % 8), device_id_type=MESH
        )
    for d in range(1, 8):
        pl.semaphore_signal(
            barrier, inc=1, device_id=(s, ((y + d) % 8) * 8 + zc), device_id_type=MESH
        )
    pl.semaphore_wait(barrier, 70)

    y_order = (4, 3, 5, 2, 6, 1, 7)
    send(q_hbm, qg.at[zc], ssem.at[0], rqs.at[zl], s, sib)
    for d in (1, 3, 2):
        send(q_hbm, qg.at[zc], ssem.at[1], rq.at[zl], s, y * 8 + ((zl + d) % 4) * 2 + c)
    for d in y_order:
        send(k_hbm, kg.at[y], ssem.at[2], rk, s, ((y + d) % 8) * 8 + zc)
    up, down = ((y + 1) % 8) * 8 + zc, ((y + 7) % 8) * 8 + zc
    for d in (1, 3, 2):
        send(v_hbm, vg.at[c, y, zl], ssem.at[3], rva.at[zl], s, y * 8 + ((zl + d) % 4) * 2 + c)
    send(v_hbm, vg.at[c, y, zl], ssem.at[13], rvr.at[0, 0, zl], s, up)
    send(v_hbm, vg.at[c, y, zl], ssem.at[13], rvr.at[1, 0, zl], s, down)

    def w_rows(shard, ch):
        return pl.ds(pl.multiple_of(shard * 288 + c * 144 + W_AT[ch], 16), W_ROWS[ch])

    def w_src(ch):
        return w3_hbm.at[pl.ds(pl.multiple_of(c * 144 + W_AT[ch], 16), W_ROWS[ch]), :]

    def w_own(ch):
        for d in (1, 3, 2):
            send(
                w_src(ch), wb.at[w_rows(s, ch), :], ssem.at[4 + ch],
                rwx.at[ch, (4 - d) % 4], ((x + d) % 4) * 2 + zh, p,
            )

    def w_over(ch):
        send(
            w_src(ch), wb.at[w_rows(s, ch), :], ssem.at[6 + ch],
            rwx.at[ch, 4], partner, p,
        )

    def w_relay(ch):
        wait(wb.at[w_rows(partner, ch), :], rwx.at[ch, 4])
        for d in (1, 3, 2):
            send(
                wb.at[w_rows(partner, ch), :], wb.at[w_rows(partner, ch), :], ssem.at[8 + ch],
                rwx.at[ch, 4 + (4 - d) % 4], ((x + d) % 4) * 2 + zh, p,
            )
        send(
            wb.at[w_rows(partner, ch), :], wb.at[w_rows(partner, ch), :], ssem.at[10],
            rww, s, sib,
        )

    def w_sibling(ch, far):
        for d in (1, 3, 2):
            shard = ((x + d) % 4) * 2 + (partner % 2 if far else zh)
            wait(wb.at[w_rows(shard, ch), :], rwx.at[ch, (4 if far else 0) + d])
            send(
                wb.at[w_rows(shard, ch), :], wb.at[w_rows(shard, ch), :], ssem.at[10],
                rww, s, sib,
            )

    for ch in range(CHUNKS):
        w_own(ch)
    w_over(0)

    part[:, 6:8, :] = jnp.zeros((64, 2, 128), F32)

    def v_unit(block, unit, way, step, target):
        send(
            vg.at[c, block, unit], vg.at[c, block, unit], ssem.at[13], rvr.at[way, step, unit], s, target
        )

    def v_sib(block):
        send(vg.at[c, block], vg.at[c, block], ssem.at[14], rvs, s, sib)

    def v_step(step):
        below, above = (y + 8 - step) % 8, (y + step) % 8
        for unit in range(4):
            wait(vg.at[0, 0, 0], rvr.at[0, step - 1, unit])
            if step < 3 or unit < 2:
                v_unit(below, unit, 0, step, up)
            wait(vg.at[0, 0, 0], rvr.at[1, step - 1, unit])
            if step < 3 or unit >= 2:
                v_unit(above, unit, 1, step, down)
        v_sib(below)
        v_sib(above)

    for d in (1, 3, 2):
        other = (zl + d) % 4
        wait(qg.at[0], rq.at[other])
        send(
            qg.at[other * 2 + c], qg.at[other * 2 + c], ssem.at[0], rqs.at[other], s, sib
        )
    loads[0].wait()
    loads[1].wait()
    for other in range(4):
        wait(qg.at[0], rqs.at[other])
    loads[2].wait()
    for d in (1, 3, 2):
        other = (zl + d) % 4
        wait(vg.at[0, 0, 0], rva.at[other])
        v_unit(y, other, 0, 0, up)
        v_unit(y, other, 1, 0, down)
    v_sib(y)
    wait(kg.at[0:7], rk)

    lane64 = lax.broadcasted_iota(jnp.int32, (64, 128), 1) < 64
    zero64 = jnp.zeros((64, 128), BF16)
    for k in range(6):
        left = jnp.concatenate([qg[:, r, k].reshape(64, 128) for r in range(4)], axis=1)
        keys = [kg[:, r, k].reshape(64, 128) for r in range(4)]
        low = jnp.concatenate([jnp.where(lane64, b, zero64) for b in keys], axis=1)
        high = jnp.concatenate([jnp.where(lane64, zero64, b) for b in keys], axis=1)
        tile = lax.dot_general(
            left, jnp.concatenate([low, high], axis=0), NT, preferred_element_type=F32
        )
        part[:, k, :] = tile

    own = pltpu.make_async_copy(part.at[zc * 8 + s], rs.at[plane], lsem.at[7])
    own.start()

    for d in range(1, 64):
        so, zo = (s + d // 8) % 8, (zc + d % 8) % 8
        send(part.at[zo * 8 + so], rs.at[plane], ssem.at[11], rrs, so, y * 8 + zo)

    for ch in range(1, CHUNKS):
        w_over(ch)
    v_step(1)
    w_relay(0)
    v_step(2)
    own.wait()
    wait(rs.at[0:63], rrs)
    logits = rs[0:8]
    for so in range(1, 8):
        logits = logits + rs[so * 8 : so * 8 + 8]
    logits = logits * (1.0 / (math.sqrt(64) * math.sqrt(32)))
    lane8 = lax.broadcasted_iota(jnp.int32, (8, 128), 1)
    lower = lane8 < 64
    peak = jnp.max(logits, axis=0)
    neg = jnp.full((8, 128), -jnp.inf, F32)
    peak_low = jnp.max(jnp.where(lower, peak, neg), axis=1, keepdims=True)
    peak_high = jnp.max(jnp.where(lower, neg, peak), axis=1, keepdims=True)
    exponent = jnp.exp(logits - jnp.where(lower, peak_low, peak_high)[None])
    total = jnp.sum(exponent, axis=0)
    zero8 = jnp.zeros((8, 128), F32)
    total_low = jnp.sum(jnp.where(lower, total, zero8), axis=1, keepdims=True)
    total_high = jnp.sum(jnp.where(lower, zero8, total), axis=1, keepdims=True)
    weights = exponent / jnp.where(lower, total_low, total_high)[None]
    for z in range(4):
        even, odd = weights[2 * z], weights[2 * z + 1]
        wm[z] = jnp.where(lower, even, pltpu.roll(odd, 64, 1)).astype(BF16)
        wm[4 + z] = jnp.where(lower, pltpu.roll(even, 64, 1), odd).astype(BF16)

    seq_order = (7, 1, 2, 6, 3, 5, 4)
    keep = pltpu.make_async_copy(wm, wg.at[s], lsem.at[8])
    keep.start()
    for d in seq_order:
        send(wm, wg.at[s], ssem.at[15], rwg, (s + d) % 8, p)
    v_step(3)
    for ch in range(1, CHUNKS):
        w_relay(ch)
    for ch in range(CHUNKS):
        w_sibling(ch, False)

    keep.wait()
    wait(wg.at[0:7], rwg)
    wf[...] = wg[...].astype(F32)

    sums = wf[0]
    for i in range(1, 8):
        sums = sums + wf[i]
    base = c * 64 + y * 8
    for hh in range(2):
        placed = zero8
        for i in range(8):
            block = wf[i, hh * 4] + wf[i, hh * 4 + 1] + wf[i, hh * 4 + 2] + wf[i, hh * 4 + 3]
            placed = placed + jnp.where(
                lane8 == base + i, jnp.sum(block, axis=1, keepdims=True), zero8
            )
        for z in range(4):
            here = (zl == z).astype(F32)
            ptl[hh * 4 + z] = sums[hh * 4 + z] + here * placed
    ptz[zc] = ptl[s]
    for d in range(1, 8):
        send(ptl.at[s], ptz.at[zc], ssem.at[16], rpz, s, y * 8 + (zc + d) % 8)

    loads[8].wait()
    for z in range(4):
        acc = zero8
        for k in range(6):
            for hh in range(2):
                acc = acc + factor_ref[2 * k + hh] * wf[:, hh * 4 + z, k, :]
        mloc[z] = acc

    @pl.when(y == s)
    def _():
        for d in y_order:
            send(mloc, mrow, ssem.at[17], rm1, s, ((y + d) % 8) * 8 + zc)

    for unit in range(4):
        wait(vg.at[0, 0, 0], rvr.at[unit // 2, 3, unit])
    opposite = (y + 4) % 8
    v_sib(opposite)
    wait(vg.at[0], rvs)

    lower16 = lax.broadcasted_iota(jnp.int32, (8, 512), 1) % 128 < 64
    mixed = []
    for k in range(6):
        left = jnp.concatenate(
            [
                jnp.concatenate([wf[:, hh * 4 + z, k, :] for z in range(4)], axis=1)
                for hh in range(2)
            ],
            axis=0,
        ).astype(BF16)
        right = jnp.concatenate(
            [
                jnp.concatenate(
                    [vg[:, :, z, r, k].reshape(128, 128) for z in range(4)], axis=0
                )
                for r in range(4)
            ],
            axis=1,
        )
        both = jnp.dot(left, right, preferred_element_type=F32)
        mixed.append(jnp.where(lower16, both[0:8], both[8:16]))
    row_out = jnp.concatenate(
        [
            jnp.concatenate([mixed[k][:, r * 128 : r * 128 + 128] for k in range(6)], axis=1)
            for r in range(4)
        ],
        axis=0,
    ).astype(BF16)
    loads[4].wait()
    loads[6].wait()
    loads[7].wait()
    skip = jnp.concatenate(
        [
            jnp.concatenate([sk[r, k].astype(F32) for k in range(6)], axis=1)
            for r in range(4)
        ],
        axis=0,
    )
    scaling = jnp.concatenate([gain[k : k + 1, :] for k in range(6)], axis=1)
    hidden = skip + jnp.dot(row_out, wc[...], preferred_element_type=F32)
    hid[...] = hidden
    average = jnp.mean(hidden, axis=1, keepdims=True)
    centered = hidden - average
    spread = jnp.mean(centered * centered, axis=1, keepdims=True)
    normed = centered * lax.rsqrt(spread + 1e-05) * scaling
    for r in range(4):
        for k in range(6):
            nf[:, r * 6 + k, :] = normed[r * 8 : r * 8 + 8, k * 128 : k * 128 + 128]
    nm[...] = nf[...].astype(BF16)
    keep = pltpu.make_async_copy(nm.at[s], ng.at[s], lsem.at[9])
    keep.start()
    for d in seq_order:
        send(nm.at[(s + d) % 8], ng.at[s], ssem.at[18], rng, (s + d) % 8, p)

    wait(ptz.at[0:7], rpz)
    acc = ptz[0]
    for z in range(1, 8):
        acc = acc + ptz[z]
    stage[0] = acc
    pty[y] = acc
    for d in y_order:
        send(stage.at[0], pty.at[y], ssem.at[19], rpy, s, ((y + d) % 8) * 8 + zc)
    for ch in range(CHUNKS):
        w_sibling(ch, True)
    loads[3].wait()
    wait(wb.at[0:1008, :], rww)

    wait(pty.at[0:7], rpy)
    acc = pty[0]
    for o in range(1, 8):
        acc = acc + pty[o]
    stage[1] = acc
    pts[s] = acc
    for d in seq_order:
        send(stage.at[1], pts.at[s], ssem.at[21], rps, (s + d) % 8, p)

    @pl.when(y == s)
    def _():
        mrow[...] = mloc[...]

    @pl.when(y != s)
    def _():
        wait(mrow, rm1)

    mcol[zc] = mrow[zl]
    for d in range(1, 8):
        o = (zc + d) % 8
        send(mrow.at[o // 2], mcol.at[zc], ssem.at[22], rm2, s, y * 8 + o)

    def unpack(ref):
        nf[...] = ref[...].astype(F32)
        return jnp.concatenate(
            [
                jnp.concatenate([nf[:, r * 6 + k, :] for k in range(6)], axis=1)
                for r in range(4)
            ],
            axis=0,
        ).astype(BF16)

    keep.wait()
    wait(ng.at[0:7], rng)
    cells = unpack(ng)
    proj[...] = lax.dot_general(cells, wb[...], NT, preferred_element_type=F32).astype(BF16)
    lane32 = lax.broadcasted_iota(jnp.int32, (32, 128), 1) < 64
    zero32 = jnp.zeros((32, 128), BF16)
    outs = []
    for k in range(6):
        cq = proj[:, k * 128 : k * 128 + 128]
        ck = proj[:, 768 + k * 128 : 768 + k * 128 + 128]
        cv = proj[:, 1536 + k * 128 : 1536 + k * 128 + 128]
        left = jnp.concatenate(
            [jnp.where(lane32, cq, zero32), jnp.where(lane32, zero32, cq)], axis=0
        )
        score = lax.dot_general(left, ck, NT, preferred_element_type=F32) * (1.0 / math.sqrt(64))
        exponent = jnp.exp(score)
        share = (exponent / jnp.sum(exponent, axis=1, keepdims=True)).astype(BF16)
        both = jnp.dot(share, cv, preferred_element_type=F32)
        outs.append(jnp.where(lane32, both[0:32], both[32:64]))
    for r in range(4):
        for k in range(6):
            nf[:, r * 6 + k, :] = outs[k][r * 8 : r * 8 + 8]
    cm[...] = nf[...].astype(BF16)
    keep = pltpu.make_async_copy(cm.at[s], cg.at[s], lsem.at[10])
    keep.start()
    for d in seq_order:
        send(cm.at[(s + d) % 8], cg.at[s], ssem.at[20], rcg, (s + d) % 8, p)

    wait(pts.at[0:7], rps)
    wait(mcol.at[0:7], rm2)
    row8 = lax.broadcasted_iota(jnp.int32, (8, 128), 0)
    scaled, cols = [], []
    for hh in range(2):
        whole = pts[hh * 4] + pts[hh * 4 + 1] + pts[hh * 4 + 2] + pts[hh * 4 + 3]
        head_total = jnp.sum(whole, axis=1, keepdims=True)
        factor = zero8
        for k in range(6):
            factor = jnp.where(row8 == k, factor_ref[2 * k + hh], factor)
        scaled.append(factor / head_total * pts[hh * 4 + zl])
    block = jnp.zeros((24, 64), F32)
    lane_at = lax.broadcasted_iota(jnp.int32, (128, 64), 0)
    col_at = lax.broadcasted_iota(jnp.int32, (128, 64), 1)
    wanted = ((col_at // 8) % 2) * 64 + s * 8 + col_at % 8
    for z in range(4):
        pick = jnp.where((lane_at == wanted) & (col_at // 16 == z), 1.0, 0.0).astype(F32)
        block = block + jnp.dot(
            jnp.concatenate([pts[z], pts[4 + z], mloc[z]], axis=0), pick,
            precision=HI, preferred_element_type=F32,
        )
    mine = jnp.where(lane8 == base + row8, 1.0, 0.0).astype(F32)
    rows_here = lax.dot_general(
        mine, jnp.concatenate(scaled, axis=0), NT, precision=HI, preferred_element_type=F32
    )
    product = jnp.dot(rows_here, block[0:16], precision=HI, preferred_element_type=F32)
    mirrored = lax.dot_general(
        mine, mcol[...].reshape(64, 128), NT, precision=HI, preferred_element_type=F32
    )
    pair_ref[...] = jax.nn.sigmoid(block[16:24] + mirrored - product + offset_ref[0])

    loads[5].wait()
    keep.wait()
    wait(cg.at[0:7], rcg)
    cells = unpack(cg)
    closing = hid[...] + jnp.dot(cells, wo[...], preferred_element_type=F32)
    for r in range(4):
        for k in range(6):
            out_ref[r, k] = closing[r * 8 : r * 8 + 8, k * 128 : k * 128 + 128].astype(BF16)

    wait(qg.at[0:4], ssem.at[0])
    wait(qg.at[0:3], ssem.at[1])
    wait(kg.at[0:7], ssem.at[2])
    wait(vg.at[0, 0, 0:3], ssem.at[3])
    for ch in range(CHUNKS):
        wait(wb.at[0 : 3 * W_ROWS[ch], :], ssem.at[4 + ch])
        wait(wb.at[0 : W_ROWS[ch], :], ssem.at[6 + ch])
        wait(wb.at[0 : 3 * W_ROWS[ch], :], ssem.at[8 + ch])
    wait(wb.at[0:1008, :], ssem.at[10])
    wait(rs.at[0:63], ssem.at[11])
    wait(vg.at[0, 0:7], ssem.at[13])
    wait(vg.at[0], ssem.at[14])
    wait(wg.at[0:7], ssem.at[15])
    wait(ptz.at[0:7], ssem.at[16])

    @pl.when(y == s)
    def _():
        wait(rs.at[0:28], ssem.at[17])

    wait(ng.at[0:7], ssem.at[18])
    wait(pty.at[0:7], ssem.at[19])
    wait(cg.at[0:7], ssem.at[20])
    wait(pts.at[0:7], ssem.at[21])
    wait(mcol.at[0:7], ssem.at[22])


def per_device(
    skip_stream_input,
    lateral_asking_vectors,
    lateral_matched_vectors,
    lateral_carried_vectors,
    lateral_closing_linear,
    upright_normalizer_multiplier,
    upright_threefold_linear,
    upright_closing_linear,
    regression_factors,
    regression_offset,
):
    def tiles(array):
        return array.reshape(4, 8, 6, 128).transpose(0, 2, 1, 3)

    def vmem(*shape, dtype=BF16):
        return pltpu.VMEM(shape, dtype)

    def dma(*shape):
        return pltpu.SemaphoreType.DMA(shape)

    anywhere = pl.BlockSpec(memory_space=pltpu.HBM)
    in_vmem = pl.BlockSpec(memory_space=pltpu.VMEM)
    one = pltpu.SemaphoreType.DMA
    aligned, pairs = pl.pallas_call(
        body,
        out_shape=(
            jax.ShapeDtypeStruct((4, 6, 8, 128), BF16),
            jax.ShapeDtypeStruct((8, 64), F32),
        ),
        in_specs=[anywhere] * 9 + [pl.BlockSpec(memory_space=pltpu.SMEM)],
        out_specs=(in_vmem, in_vmem),
        scratch_shapes=[
            vmem(8, 4, 6, 8, 128),
            vmem(8, 4, 6, 8, 128),
            vmem(2, 8, 4, 4, 6, 8, 128),
            vmem(2304, 768),
            vmem(768, 768),
            vmem(768, 768),
            vmem(4, 6, 8, 128),
            vmem(64, 8, 128, dtype=F32),
            vmem(64, 8, 128, dtype=F32),
            vmem(8, 8, 128),
            vmem(8, 8, 8, 128),
            vmem(8, 8, 8, 128, dtype=F32),
            vmem(8, 24, 128, dtype=F32),
            vmem(8, 24, 128),
            vmem(8, 24, 128),
            vmem(8, 24, 128),
            vmem(8, 24, 128),
            vmem(32, 768, dtype=F32),
            vmem(32, 2304),
            vmem(6, 128, dtype=F32),
            pltpu.SMEM((12,), F32),
            vmem(8, 8, 128, dtype=F32),
            vmem(8, 8, 128, dtype=F32),
            vmem(8, 8, 128, dtype=F32),
            vmem(8, 8, 128, dtype=F32),
            vmem(4, 8, 128, dtype=F32),
            vmem(4, 8, 128, dtype=F32),
            vmem(8, 8, 128, dtype=F32),
            vmem(2, 8, 128, dtype=F32),
            dma(14),
            dma(23),
            dma(4),
            dma(4),
            one,
            dma(4),
            one,
            dma(2, 4, 4),
            dma(CHUNKS, 8),
            one,
            one,
            one,
            one,
            one,
            one,
            one,
            one,
            one,
            one,
        ],
        compiler_params=pltpu.CompilerParams(
            collective_id=0, has_side_effects=True, vmem_limit_bytes=62 << 20
        ),
        name="axial_layer",
    )(
        tiles(skip_stream_input),
        tiles(lateral_asking_vectors),
        tiles(lateral_matched_vectors),
        tiles(lateral_carried_vectors),
        lateral_closing_linear,
        upright_normalizer_multiplier.reshape(6, 128),
        upright_threefold_linear.T,
        upright_closing_linear,
        regression_factors,
        regression_offset,
    )
    return aligned.transpose(0, 2, 1, 3).reshape(4, 8, 768), pairs


def solution(mesh):
    placed = (
        P("seq", "pos", None),
        P("seq", "pos", None),
        P("seq", "pos", None),
        P("seq", "pos", None),
        P(),
        P(),
        P(None, "seq"),
        P(),
        P(),
        P(),
    )
    return jax.shard_map(
        per_device,
        mesh=mesh,
        in_specs=placed,
        out_specs=(P("seq", "pos", None), P("pos", "seq")),
        check_vma=False,
    )
```

```python
import math

import jax
import jax.numpy as jnp
from jax import lax
from jax.experimental import pallas as pl
from jax.experimental.pallas import tpu as pltpu
from jax.sharding import PartitionSpec as P

MESH = pl.DeviceIdType.MESH
HI = lax.Precision.HIGHEST
F32 = jnp.float32
BF16 = jnp.bfloat16
NT = (((1,), (1,)), ((), ()))


def body(
    skip_hbm, q_hbm, k_hbm, v_hbm, wc_hbm, gain_hbm, w3_hbm, wo_hbm, factor_hbm, offset_ref,
    out_ref, pair_ref,
    qg, kg, vg, wb, wc, wo, sk,
    part, rs, wm, wg, wf, nf, nm, ng, cm, cg, gf, cf, hid, proj, gain, factor_ref,
    ptl, ptz, pty, pts, mloc, mrow, mcol, stage,
    lsem, ssem, rq, rqs, rk, rva, rvs, rvr, rw, rww, wlocal, wsu, wsf, wss, rrs, rwg, rng, rcg, rpz, rpy, rps, rm1, rm2,
):
    s = lax.axis_index("seq")
    p = lax.axis_index("pos")
    x, zh = s // 2, s % 2
    y, zc = p // 8, p % 8
    zl, c = zc // 2, zc % 2
    sib = y * 8 + zl * 2 + (1 - c)

    def local(src, dst, index):
        copy = pltpu.make_async_copy(src, dst, lsem.at[index])
        copy.start()
        return copy

    def send(src, dst, send_sem, recv_sem, seq, pos):
        pltpu.make_async_remote_copy(
            src_ref=src, dst_ref=dst, send_sem=send_sem, recv_sem=recv_sem,
            device_id=(seq, pos), device_id_type=MESH,
        ).start()

    def wait(ref, sem):
        pltpu.make_async_copy(ref, ref, sem).wait()

    barrier = pltpu.get_barrier_semaphore()
    plane = s * 8 + zc
    for d in (4, 3, 5, 2, 6, 1, 7):
        for peer in (((s + d) % 8, p), (s, ((y + d) % 8) * 8 + zc), (s, y * 8 + (zc + d) % 8)):
            pl.semaphore_signal(barrier, inc=1, device_id=peer, device_id_type=MESH)
    loads = [
        local(q_hbm, qg.at[zc], 0),
        local(k_hbm, kg.at[y], 1),
        local(v_hbm, vg.at[c, y, zl], 2),
        None,
        local(wc_hbm, wc, 4),
        local(wo_hbm, wo, 5),
        local(skip_hbm, sk, 6),
        local(gain_hbm, gain, 11),
        local(factor_hbm, factor_ref, 12),
    ]
    pl.semaphore_wait(barrier, 21)

    y_order = (4, 3, 5, 2, 6, 1, 7)
    up, down = ((y + 1) % 8) * 8 + zc, ((y + 7) % 8) * 8 + zc
    z_order = (2, 1, 3)
    for d in z_order:
        send(q_hbm, qg.at[zc], ssem.at[1], rq.at[zl], s, y * 8 + ((zl + d) % 4) * 2 + c)
    send(q_hbm, qg.at[zc], ssem.at[0], rqs.at[zl], s, sib)
    for d in z_order:
        send(v_hbm, vg.at[c, y, zl], ssem.at[3], rva.at[zl], s, y * 8 + ((zl + d) % 4) * 2 + c)
    for d in y_order:
        send(k_hbm, kg.at[y], ssem.at[2], rk, s, ((y + d) % 8) * 8 + zc)
    send(v_hbm, vg.at[c, y, zl], ssem.at[13], rvr.at[0, 0, zl], s, up)
    send(v_hbm, vg.at[c, y, zl], ssem.at[13], rvr.at[1, 0, zl], s, down)

    def x_peers(src, dst, send_sem, recv_sem):
        for d in (2, 1, 3):
            send(src, dst, send_sem, recv_sem, ((x + d) % 4) * 2 + zh, p)

    def w_unit(u):
        col = s * 288 + 32 * u
        role, within = col // 768, col % 768
        pair = within // 128
        index = role * 12 + (pair // 2) * 4 + (within % 128) // 32
        src = w3_hbm.at[pl.ds(pl.multiple_of(32 * u + c * 16, 16), 16), :]
        dst = wb.at[pl.ds(pl.multiple_of(index * 32 + c * 16, 16), 16), :]
        return pair % 2, index, src, dst

    def w_near(u):
        group, index, src, dst = w_unit(u)

        @pl.when(group == zh)
        def _():
            pltpu.make_async_copy(src, dst, wlocal.at[u]).start()
            x_peers(src, dst, wsu.at[u], rw.at[index])
            send(src, dst, wsu.at[u], rww, s, sib)

    def w_far(u):
        group, index, src, dst = w_unit(u)

        @pl.when(group != zh)
        def _():
            send(src, dst, wsu.at[u], rw.at[index], x * 2 + 1 - zh, p)

    def w_place(n):
        col = (n // 12) * 768 + (n % 12 // 4) * 256 + zh * 128 + (n % 4) * 32
        owner = col // 288
        here = owner // 2 == x
        far = owner % 2 != zh
        return far & here, jnp.logical_not(far) & here, wb.at[pl.ds(pl.multiple_of(n * 32 + c * 16, 16), 16), :]

    def w_pass(n):
        lands, mine, dst = w_place(n)

        @pl.when(lands)
        def _():
            wait(dst, rw.at[n])
            x_peers(dst, dst, wsf.at[n], rw.at[n])
            send(dst, dst, wss.at[n], rww, s, sib)

    def w_last(n):
        lands, mine, dst = w_place(n)

        @pl.when(jnp.logical_not(lands | mine))
        def _():
            wait(dst, rw.at[n])
            send(dst, dst, wss.at[n], rww, s, sib)

    for u in range(9):
        w_near(u)

    rs[:, 6:8, :] = jnp.zeros((64, 2, 128), F32)
    wg[:, :, 6:8, :] = jnp.zeros((8, 8, 2, 128), BF16)

    def v_unit(block, unit, way, step, target):
        send(
            vg.at[c, block, unit], vg.at[c, block, unit], ssem.at[13], rvr.at[way, step, unit], s, target
        )

    def v_sib(block):
        send(vg.at[c, block], vg.at[c, block], ssem.at[14], rvs, s, sib)

    v_order = (0, 1, 3, 2)

    def v_step(step, places):
        below, above = (y + 8 - step) % 8, (y + step) % 8
        for at in places:
            unit = (zl + v_order[at]) % 4
            wait(vg.at[0, 0, 0], rvr.at[0, step - 1, unit])
            if step < 3 or at < 2:
                v_unit(below, unit, 0, step, up)
            wait(vg.at[0, 0, 0], rvr.at[1, step - 1, unit])
            if step < 3 or at >= 2:
                v_unit(above, unit, 1, step, down)
        if 3 in places:
            v_sib(below)
            v_sib(above)

    for d in (1, 3, 2):
        other = (zl + d) % 4
        wait(qg.at[0], rq.at[other])
        send(
            qg.at[other * 2 + c], qg.at[other * 2 + c], ssem.at[0], rqs.at[other], s, sib
        )
    loads[0].wait()
    loads[1].wait()
    for other in range(4):
        wait(qg.at[0], rqs.at[other])
    for u in range(9):
        w_far(u)
    wait(kg.at[0:7], rk)

    lane64 = lax.broadcasted_iota(jnp.int32, (64, 128), 1) < 64
    zero64 = jnp.zeros((64, 128), BF16)
    for k in range(6):
        left = jnp.concatenate([qg[:, r, k].reshape(64, 128) for r in range(4)], axis=1)
        keys = [kg[:, r, k].reshape(64, 128) for r in range(4)]
        low = jnp.concatenate([jnp.where(lane64, b, zero64) for b in keys], axis=1)
        high = jnp.concatenate([jnp.where(lane64, zero64, b) for b in keys], axis=1)
        tile = lax.dot_general(
            left, jnp.concatenate([low, high], axis=0), NT, preferred_element_type=F32
        )
        part[:, k, :] = tile

    own = pltpu.make_async_copy(part.at[zc * 8 + s, 0:6], rs.at[plane, 0:6], lsem.at[7])
    own.start()

    for d in range(1, 64):
        so, zo = (s + d // 8) % 8, (zc + d % 8) % 8
        send(part.at[zo * 8 + so, 0:6], rs.at[plane, 0:6], ssem.at[11], rrs, so, y * 8 + zo)

    loads[2].wait()
    for d in (1, 3, 2):
        other = (zl + d) % 4
        wait(vg.at[0, 0, 0], rva.at[other])
        v_unit(y, other, 0, 0, up)
        v_unit(y, other, 1, 0, down)
    v_sib(y)
    v_step(1, (0, 1, 2, 3))
    for n in range(36):
        w_pass(n)
    v_step(2, (0, 1, 2, 3))
    own.wait()
    wait(rs.at[0:63, 0:6], rrs)
    logits = rs[0:8]
    for so in range(1, 8):
        logits = logits + rs[so * 8 : so * 8 + 8]
    logits = logits * (1.0 / (math.sqrt(64) * math.sqrt(32)))
    lane8 = lax.broadcasted_iota(jnp.int32, (8, 128), 1)
    lower = lane8 < 64
    peak = jnp.max(logits, axis=0)
    neg = jnp.full((8, 128), -jnp.inf, F32)
    peak_low = jnp.max(jnp.where(lower, peak, neg), axis=1, keepdims=True)
    peak_high = jnp.max(jnp.where(lower, neg, peak), axis=1, keepdims=True)
    exponent = jnp.exp(logits - jnp.where(lower, peak_low, peak_high)[None])
    total = jnp.sum(exponent, axis=0)
    zero8 = jnp.zeros((8, 128), F32)
    total_low = jnp.sum(jnp.where(lower, total, zero8), axis=1, keepdims=True)
    total_high = jnp.sum(jnp.where(lower, zero8, total), axis=1, keepdims=True)
    weights = exponent / jnp.where(lower, total_low, total_high)[None]
    for z in range(4):
        even, odd = weights[2 * z], weights[2 * z + 1]
        wm[z] = jnp.where(lower, even, pltpu.roll(odd, 64, 1)).astype(BF16)
        wm[4 + z] = jnp.where(lower, pltpu.roll(even, 64, 1), odd).astype(BF16)

    seq_order = (7, 1, 2, 6, 3, 5, 4)
    keep = pltpu.make_async_copy(wm.at[:, 0:6], wg.at[s, :, 0:6], lsem.at[8])
    keep.start()
    for d in seq_order:
        send(wm.at[:, 0:6], wg.at[s, :, 0:6], ssem.at[15], rwg, (s + d) % 8, p)
    v_step(3, (0, 1, 2, 3))
    for n in range(36):
        w_last(n)
    keep.wait()
    wait(wg.at[0:7, :, 0:6], rwg)
    wf[...] = wg[...].astype(F32)

    sums = wf[0]
    for i in range(1, 8):
        sums = sums + wf[i]
    base = c * 64 + y * 8
    for hh in range(2):
        placed = zero8
        for i in range(8):
            block = wf[i, hh * 4] + wf[i, hh * 4 + 1] + wf[i, hh * 4 + 2] + wf[i, hh * 4 + 3]
            placed = placed + jnp.where(
                lane8 == base + i, jnp.sum(block, axis=1, keepdims=True), zero8
            )
        for z in range(4):
            here = (zl == z).astype(F32)
            ptl[hh * 4 + z] = sums[hh * 4 + z] + here * placed
    ptz[zc] = ptl[s]
    for d in range(1, 8):
        send(ptl.at[s], ptz.at[zc], ssem.at[16], rpz, s, y * 8 + (zc + d) % 8)

    loads[8].wait()
    for z in range(4):
        acc = zero8
        for k in range(6):
            for hh in range(2):
                acc = acc + factor_ref[2 * k + hh] * wf[:, hh * 4 + z, k, :]
        mloc[z] = acc

    @pl.when(y == s)
    def _():
        for d in y_order:
            send(mloc, mrow, ssem.at[17], rm1, s, ((y + d) % 8) * 8 + zc)

    for at in range(4):
        wait(vg.at[0, 0, 0], rvr.at[at // 2, 3, (zl + v_order[at]) % 4])
    opposite = (y + 4) % 8
    v_sib(opposite)
    wait(vg.at[0], rvs)

    lower16 = lax.broadcasted_iota(jnp.int32, (8, 512), 1) % 128 < 64
    mixed = []
    for k in range(6):
        left = jnp.concatenate(
            [
                jnp.concatenate([wf[:, hh * 4 + z, k, :] for z in range(4)], axis=1)
                for hh in range(2)
            ],
            axis=0,
        ).astype(BF16)
        right = jnp.concatenate(
            [
                jnp.concatenate(
                    [vg[:, :, z, r, k].reshape(128, 128) for z in range(4)], axis=0
                )
                for r in range(4)
            ],
            axis=1,
        )
        both = jnp.dot(left, right, preferred_element_type=F32)
        mixed.append(jnp.where(lower16, both[0:8], both[8:16]))
    row_out = jnp.concatenate(
        [
            jnp.concatenate([mixed[k][:, r * 128 : r * 128 + 128] for k in range(6)], axis=1)
            for r in range(4)
        ],
        axis=0,
    ).astype(BF16)
    loads[4].wait()
    loads[6].wait()
    loads[7].wait()
    skip = jnp.concatenate(
        [
            jnp.concatenate([sk[r, k].astype(F32) for k in range(6)], axis=1)
            for r in range(4)
        ],
        axis=0,
    )
    scaling = jnp.concatenate([gain[k : k + 1, :] for k in range(6)], axis=1)
    hidden = skip + jnp.dot(row_out, wc[...], preferred_element_type=F32)
    hid[...] = hidden
    average = jnp.mean(hidden, axis=1, keepdims=True)
    centered = hidden - average
    spread = jnp.mean(centered * centered, axis=1, keepdims=True)
    normed = centered * lax.rsqrt(spread + 1e-05) * scaling
    for r in range(4):
        for k in range(6):
            nf[:, r * 6 + k, :] = normed[r * 8 : r * 8 + 8, k * 128 : k * 128 + 128]
    nm[:, 0] = nf[0:4].astype(BF16)
    nm[:, 1] = nf[4:8].astype(BF16)
    keep = pltpu.make_async_copy(nm.at[x], ng.at[s], lsem.at[9])
    keep.start()
    for d in seq_order:
        send(nm.at[((s + d) % 8) // 2], ng.at[s], ssem.at[18], rng, (s + d) % 8, p)

    wait(ptz.at[0:7], rpz)
    acc = ptz[0]
    for z in range(1, 8):
        acc = acc + ptz[z]
    stage[0] = acc
    pty[y] = acc
    for d in y_order:
        send(stage.at[0], pty.at[y], ssem.at[19], rpy, s, ((y + d) % 8) * 8 + zc)
    for u in range(9):
        group, index, src, dst = w_unit(u)

        @pl.when(group == zh)
        def _():
            pltpu.make_async_copy(src, dst, wlocal.at[u]).wait()

    wait(wb.at[0:576, :], rww)

    wait(pty.at[0:7], rpy)
    acc = pty[0]
    for o in range(1, 8):
        acc = acc + pty[o]
    stage[1] = acc
    pts[s] = acc
    for d in seq_order:
        send(stage.at[1], pts.at[s], ssem.at[21], rps, (s + d) % 8, p)

    @pl.when(y == s)
    def _():
        mrow[...] = mloc[...]

    @pl.when(y != s)
    def _():
        wait(mrow, rm1)

    mcol[zc] = mrow[zl]
    for d in range(1, 8):
        o = (zc + d) % 8
        send(mrow.at[o // 2], mcol.at[zc], ssem.at[22], rm2, s, y * 8 + o)

    keep.wait()
    wait(ng.at[0:7], rng)
    gf[...] = ng[...].astype(F32)
    cells = jnp.concatenate(
        [
            jnp.concatenate([gf[:, b, r * 6 + k, :] for k in range(6)], axis=1)
            for r in range(4)
            for b in range(2)
        ],
        axis=0,
    ).astype(BF16)
    proj[...] = lax.dot_general(cells, wb[...], NT, preferred_element_type=F32).astype(BF16)
    lane_low = lax.broadcasted_iota(jnp.int32, (64, 128), 1) < 64
    same = (
        lax.broadcasted_iota(jnp.int32, (128, 64), 0) // 8 % 2
        == lax.broadcasted_iota(jnp.int32, (128, 64), 1) // 8 % 2
    )
    for k in range(3):
        cq = proj[:, k * 128 : k * 128 + 128]
        ck = proj[:, 384 + k * 128 : 384 + k * 128 + 128]
        cv = proj[:, 768 + k * 128 : 768 + k * 128 + 128]
        left = jnp.concatenate(
            [jnp.where(lane_low, cq, zero64), jnp.where(lane_low, zero64, cq)], axis=0
        )
        score = lax.dot_general(left, ck, NT, preferred_element_type=F32) * (1.0 / math.sqrt(64))
        exponent = jnp.where(same, jnp.exp(score), 0.0)
        share = (exponent / jnp.sum(exponent, axis=1, keepdims=True)).astype(BF16)
        both = jnp.dot(share, cv, preferred_element_type=F32)
        mix = jnp.where(lane_low, both[0:64], both[64:128])
        for r in range(4):
            for b in range(2):
                nf[:, b * 12 + r * 3 + k, :] = mix[r * 16 + b * 8 : r * 16 + b * 8 + 8]
    cm[...] = nf[...].astype(BF16)
    keep = pltpu.make_async_copy(cm.at[s], cg.at[zh, x], lsem.at[10])
    keep.start()
    for d in seq_order:
        send(cm.at[(s + d) % 8], cg.at[zh, x], ssem.at[20], rcg, (s + d) % 8, p)

    wait(pts.at[0:7], rps)
    wait(mcol.at[0:7], rm2)
    row8 = lax.broadcasted_iota(jnp.int32, (8, 128), 0)
    scaled, cols = [], []
    for hh in range(2):
        whole = pts[hh * 4] + pts[hh * 4 + 1] + pts[hh * 4 + 2] + pts[hh * 4 + 3]
        head_total = jnp.where(row8 < 6, jnp.sum(whole, axis=1, keepdims=True), 1.0)
        factor = zero8
        for k in range(6):
            factor = jnp.where(row8 == k, factor_ref[2 * k + hh], factor)
        scaled.append(factor / head_total * pts[hh * 4 + zl])
    block = jnp.zeros((24, 64), F32)
    lane_at = lax.broadcasted_iota(jnp.int32, (128, 64), 0)
    col_at = lax.broadcasted_iota(jnp.int32, (128, 64), 1)
    wanted = ((col_at // 8) % 2) * 64 + s * 8 + col_at % 8
    for z in range(4):
        pick = jnp.where((lane_at == wanted) & (col_at // 16 == z), 1.0, 0.0).astype(F32)
        block = block + jnp.dot(
            jnp.concatenate([pts[z], pts[4 + z], mloc[z]], axis=0), pick,
            precision=HI, preferred_element_type=F32,
        )
    mine = jnp.where(lane8 == base + row8, 1.0, 0.0).astype(F32)
    rows_here = lax.dot_general(
        mine, jnp.concatenate(scaled, axis=0), NT, precision=HI, preferred_element_type=F32
    )
    product = jnp.dot(rows_here, block[0:16], precision=HI, preferred_element_type=F32)
    mirrored = lax.dot_general(
        mine, mcol[...].reshape(64, 128), NT, precision=HI, preferred_element_type=F32
    )
    pair_ref[...] = jax.nn.sigmoid(block[16:24] + mirrored - product + offset_ref[0])

    loads[5].wait()
    keep.wait()
    wait(cm.at[0:7], rcg)
    cf[...] = cg[...].astype(F32)
    cells = jnp.concatenate(
        [
            jnp.concatenate(
                [
                    jnp.concatenate(
                        [cf[k % 2, :, b * 12 + r * 3 + k // 2, :] for b in range(2)], axis=0
                    )
                    for k in range(6)
                ],
                axis=1,
            )
            for r in range(4)
        ],
        axis=0,
    ).astype(BF16)
    closing = hid[...] + jnp.dot(cells, wo[...], preferred_element_type=F32)
    for r in range(4):
        for k in range(6):
            out_ref[r, k] = closing[r * 8 : r * 8 + 8, k * 128 : k * 128 + 128].astype(BF16)

    wait(qg.at[0:4], ssem.at[0])
    wait(qg.at[0:3], ssem.at[1])
    wait(kg.at[0:7], ssem.at[2])
    wait(vg.at[0, 0, 0:3], ssem.at[3])
    for u in range(9):
        group = w_unit(u)[0]

        @pl.when(group == zh)
        def _():
            wait(wb.at[0:64, :], wsu.at[u])

        @pl.when(group != zh)
        def _():
            wait(wb.at[0:16, :], wsu.at[u])

    for n in range(36):
        lands, mine, dst = w_place(n)

        @pl.when(lands)
        def _():
            wait(wb.at[0:48, :], wsf.at[n])

        @pl.when(jnp.logical_not(mine))
        def _():
            wait(wb.at[0:16, :], wss.at[n])

    wait(rs.at[0:63, 0:6], ssem.at[11])
    wait(vg.at[0, 0:7], ssem.at[13])
    wait(vg.at[0], ssem.at[14])
    wait(wg.at[0:7, :, 0:6], ssem.at[15])
    wait(ptz.at[0:7], ssem.at[16])

    @pl.when(y == s)
    def _():
        wait(rs.at[0:28], ssem.at[17])

    wait(ng.at[0:7], ssem.at[18])
    wait(pty.at[0:7], ssem.at[19])
    wait(cm.at[0:7], ssem.at[20])
    wait(pts.at[0:7], ssem.at[21])
    wait(mcol.at[0:7], ssem.at[22])


def per_device(
    skip_stream_input,
    lateral_asking_vectors,
    lateral_matched_vectors,
    lateral_carried_vectors,
    lateral_closing_linear,
    upright_normalizer_multiplier,
    upright_threefold_linear,
    upright_closing_linear,
    regression_factors,
    regression_offset,
):
    def tiles(array):
        return array.reshape(4, 8, 6, 128).transpose(0, 2, 1, 3)

    def vmem(*shape, dtype=BF16):
        return pltpu.VMEM(shape, dtype)

    def dma(*shape):
        return pltpu.SemaphoreType.DMA(shape)

    anywhere = pl.BlockSpec(memory_space=pltpu.HBM)
    in_vmem = pl.BlockSpec(memory_space=pltpu.VMEM)
    one = pltpu.SemaphoreType.DMA
    aligned, pairs = pl.pallas_call(
        body,
        out_shape=(
            jax.ShapeDtypeStruct((4, 6, 8, 128), BF16),
            jax.ShapeDtypeStruct((8, 64), F32),
        ),
        in_specs=[anywhere] * 9 + [pl.BlockSpec(memory_space=pltpu.SMEM)],
        out_specs=(in_vmem, in_vmem),
        scratch_shapes=[
            vmem(8, 4, 6, 8, 128),
            vmem(8, 4, 6, 8, 128),
            vmem(2, 8, 4, 4, 6, 8, 128),
            vmem(1152, 768),
            vmem(768, 768),
            vmem(768, 768),
            vmem(4, 6, 8, 128),
            vmem(64, 8, 128, dtype=F32),
            vmem(64, 8, 128, dtype=F32),
            vmem(8, 8, 128),
            vmem(8, 8, 8, 128),
            vmem(8, 8, 8, 128, dtype=F32),
            vmem(8, 24, 128, dtype=F32),
            vmem(4, 2, 24, 128),
            vmem(8, 2, 24, 128),
            vmem(8, 24, 128),
            vmem(2, 4, 24, 128),
            vmem(8, 2, 24, 128, dtype=F32),
            vmem(2, 4, 24, 128, dtype=F32),
            vmem(32, 768, dtype=F32),
            vmem(64, 1152),
            vmem(6, 128, dtype=F32),
            pltpu.SMEM((12,), F32),
            vmem(8, 8, 128, dtype=F32),
            vmem(8, 8, 128, dtype=F32),
            vmem(8, 8, 128, dtype=F32),
            vmem(8, 8, 128, dtype=F32),
            vmem(4, 8, 128, dtype=F32),
            vmem(4, 8, 128, dtype=F32),
            vmem(8, 8, 128, dtype=F32),
            vmem(2, 8, 128, dtype=F32),
            dma(14),
            dma(23),
            dma(4),
            dma(4),
            one,
            dma(4),
            one,
            dma(2, 4, 4),
            dma(36),
            one,
            dma(9),
            dma(9),
            dma(36),
            dma(36),
            one,
            one,
            one,
            one,
            one,
            one,
            one,
            one,
            one,
        ],
        compiler_params=pltpu.CompilerParams(
            collective_id=0, has_side_effects=True, vmem_limit_bytes=62 << 20
        ),
        name="axial_layer",
    )(
        tiles(skip_stream_input),
        tiles(lateral_asking_vectors),
        tiles(lateral_matched_vectors),
        tiles(lateral_carried_vectors),
        lateral_closing_linear,
        upright_normalizer_multiplier.reshape(6, 128),
        upright_threefold_linear.T,
        upright_closing_linear,
        regression_factors,
        regression_offset,
    )
    return aligned.transpose(0, 2, 1, 3).reshape(4, 8, 768), pairs


def solution(mesh):
    placed = (
        P("seq", "pos", None),
        P("seq", "pos", None),
        P("seq", "pos", None),
        P("seq", "pos", None),
        P(),
        P(),
        P(None, "seq"),
        P(),
        P(),
        P(),
    )
    return jax.shard_map(
        per_device,
        mesh=mesh,
        in_specs=placed,
        out_specs=(P("seq", "pos", None), P("pos", "seq")),
        check_vma=False,
    )
```

```python
import math

import jax
import jax.numpy as jnp
from jax import lax
from jax.experimental import pallas as pl
from jax.experimental.pallas import tpu as pltpu
from jax.sharding import PartitionSpec as P

MESH = pl.DeviceIdType.MESH
HI = lax.Precision.HIGHEST
F32 = jnp.float32
BF16 = jnp.bfloat16
NT = (((1,), (1,)), ((), ()))


def body(
    skip_hbm, q_hbm, k_hbm, v_hbm, wc_hbm, gain_hbm, w3_hbm, wo_hbm, factor_hbm, offset_ref,
    out_ref, pair_ref,
    qg, kg, vg, wb, wc, wo, sk,
    part, rs, wm, wg, wf, nf, nm, ng, cm, cg, gf, cf, hid, proj, gain, factor_ref,
    ptl, ptz, pty, pts, mloc, mrow, mcol, stage,
    lsem, ssem, rq, rqs, rk, rva, rvs, rvr, rw, rww, wlocal, wsu, wsf, wss, rrs, rwg, rng, rcg, rpz, rpy, rps, rm1, rm2,
):
    s = lax.axis_index("seq")
    p = lax.axis_index("pos")
    x, zh = s // 2, s % 2
    y, zc = p // 8, p % 8
    zl, c = zc // 2, zc % 2
    sib = y * 8 + zl * 2 + (1 - c)

    def local(src, dst, index):
        copy = pltpu.make_async_copy(src, dst, lsem.at[index])
        copy.start()
        return copy

    def send(src, dst, send_sem, recv_sem, seq, pos):
        pltpu.make_async_remote_copy(
            src_ref=src, dst_ref=dst, send_sem=send_sem, recv_sem=recv_sem,
            device_id=(seq, pos), device_id_type=MESH,
        ).start()

    def wait(ref, sem):
        pltpu.make_async_copy(ref, ref, sem).wait()

    barrier = pltpu.get_barrier_semaphore()
    plane = s * 8 + zc
    for d in (4, 3, 5, 2, 6, 1, 7):
        for peer in (((s + d) % 8, p), (s, ((y + d) % 8) * 8 + zc), (s, y * 8 + (zc + d) % 8)):
            pl.semaphore_signal(barrier, inc=1, device_id=peer, device_id_type=MESH)
    loads = [
        local(q_hbm, qg.at[zc], 0),
        local(k_hbm, kg.at[y], 1),
        local(v_hbm, vg.at[c, y, zl], 2),
        None,
        local(wc_hbm, wc, 4),
        local(wo_hbm, wo, 5),
        local(skip_hbm, sk, 6),
        local(gain_hbm, gain, 11),
        local(factor_hbm, factor_ref, 12),
    ]
    pl.semaphore_wait(barrier, 21)

    y_order = (4, 3, 5, 2, 6, 1, 7)
    up, down = ((y + 1) % 8) * 8 + zc, ((y + 7) % 8) * 8 + zc
    z_order = (2, 1, 3)
    for d in z_order:
        send(q_hbm, qg.at[zc], ssem.at[1], rq.at[zl], s, y * 8 + ((zl + d) % 4) * 2 + c)
    send(q_hbm, qg.at[zc], ssem.at[0], rqs.at[zl], s, sib)
    for d in z_order:
        send(v_hbm, vg.at[c, y, zl], ssem.at[3], rva.at[zl], s, y * 8 + ((zl + d) % 4) * 2 + c)
    for d in y_order:
        send(k_hbm, kg.at[y], ssem.at[2], rk, s, ((y + d) % 8) * 8 + zc)

    def x_peers(src, dst, send_sem, recv_sem):
        for d in (2, 1, 3):
            send(src, dst, send_sem, recv_sem, ((x + d) % 4) * 2 + zh, p)

    def w_unit(u):
        col = s * 288 + 32 * u
        role, within = col // 768, col % 768
        pair = within // 128
        index = role * 12 + (pair // 2) * 4 + (within % 128) // 32
        src = w3_hbm.at[pl.ds(pl.multiple_of(32 * u + c * 16, 16), 16), :]
        dst = wb.at[pl.ds(pl.multiple_of(index * 32 + c * 16, 16), 16), :]
        return pair % 2, index, src, dst

    def w_near(u):
        group, index, src, dst = w_unit(u)

        @pl.when(group == zh)
        def _():
            pltpu.make_async_copy(src, dst, wlocal.at[u]).start()
            x_peers(src, dst, wsu.at[u], rw.at[index])
            send(src, dst, wsu.at[u], rww, s, sib)

    def w_far(u):
        group, index, src, dst = w_unit(u)

        @pl.when(group != zh)
        def _():
            send(src, dst, wsu.at[u], rw.at[index], x * 2 + 1 - zh, p)

    def w_place(n):
        col = (n // 12) * 768 + (n % 12 // 4) * 256 + zh * 128 + (n % 4) * 32
        owner = col // 288
        here = owner // 2 == x
        far = owner % 2 != zh
        return far & here, jnp.logical_not(far) & here, wb.at[pl.ds(pl.multiple_of(n * 32 + c * 16, 16), 16), :]

    def w_pass(n):
        lands, mine, dst = w_place(n)

        @pl.when(lands)
        def _():
            wait(dst, rw.at[n])
            x_peers(dst, dst, wsf.at[n], rw.at[n])
            send(dst, dst, wss.at[n], rww, s, sib)

    def w_last(n):
        lands, mine, dst = w_place(n)

        @pl.when(jnp.logical_not(lands | mine))
        def _():
            wait(dst, rw.at[n])
            send(dst, dst, wss.at[n], rww, s, sib)

    for u in range(9):
        w_near(u)

    rs[:, 6:8, :] = jnp.zeros((64, 2, 128), F32)
    wg[:, :, 6:8, :] = jnp.zeros((8, 8, 2, 128), BF16)

    def v_unit(block, unit, way, step, target):
        send(
            vg.at[c, block, unit], vg.at[c, block, unit], ssem.at[13], rvr.at[way, step, unit], s, target
        )

    def v_sib(block):
        send(vg.at[c, block], vg.at[c, block], ssem.at[14], rvs, s, sib)

    v_order = (0, 1, 3, 2)

    def v_step(step, places):
        below, above = (y + 8 - step) % 8, (y + step) % 8
        for at in places:
            unit = (zl + v_order[at]) % 4
            wait(vg.at[0, 0, 0], rvr.at[0, step - 1, unit])
            if step < 3 or at < 2:
                v_unit(below, unit, 0, step, up)
            wait(vg.at[0, 0, 0], rvr.at[1, step - 1, unit])
            if step < 3 or at >= 2:
                v_unit(above, unit, 1, step, down)
        if 3 in places:
            v_sib(below)
            v_sib(above)

    for d in (1, 3, 2):
        other = (zl + d) % 4
        wait(qg.at[0], rq.at[other])
        send(
            qg.at[other * 2 + c], qg.at[other * 2 + c], ssem.at[0], rqs.at[other], s, sib
        )
    loads[0].wait()
    loads[1].wait()
    for other in range(4):
        wait(qg.at[0], rqs.at[other])
    send(v_hbm, vg.at[c, y, zl], ssem.at[13], rvr.at[0, 0, zl], s, up)
    send(v_hbm, vg.at[c, y, zl], ssem.at[13], rvr.at[1, 0, zl], s, down)
    for u in range(9):
        w_far(u)
    wait(kg.at[0:7], rk)

    lane64 = lax.broadcasted_iota(jnp.int32, (64, 128), 1) < 64
    zero64 = jnp.zeros((64, 128), BF16)
    for k in range(6):
        left = jnp.concatenate([qg[:, r, k].reshape(64, 128) for r in range(4)], axis=1)
        keys = [kg[:, r, k].reshape(64, 128) for r in range(4)]
        low = jnp.concatenate([jnp.where(lane64, b, zero64) for b in keys], axis=1)
        high = jnp.concatenate([jnp.where(lane64, zero64, b) for b in keys], axis=1)
        tile = lax.dot_general(
            left, jnp.concatenate([low, high], axis=0), NT, preferred_element_type=F32
        )
        part[:, k, :] = tile

    own = pltpu.make_async_copy(part.at[zc * 8 + s, 0:6], rs.at[plane, 0:6], lsem.at[7])
    own.start()

    for d in range(1, 64):
        so, zo = (s + d // 8) % 8, (zc + d % 8) % 8
        send(part.at[zo * 8 + so, 0:6], rs.at[plane, 0:6], ssem.at[11], rrs, so, y * 8 + zo)

    loads[2].wait()
    for d in (1, 3, 2):
        other = (zl + d) % 4
        wait(vg.at[0, 0, 0], rva.at[other])
        v_unit(y, other, 0, 0, up)
        v_unit(y, other, 1, 0, down)
    v_sib(y)
    v_step(1, (0, 1, 2, 3))
    v_step(2, (0, 1))
    own.wait()
    wait(rs.at[0:63, 0:6], rrs)
    logits = rs[0:8]
    for so in range(1, 8):
        logits = logits + rs[so * 8 : so * 8 + 8]
    logits = logits * (1.0 / (math.sqrt(64) * math.sqrt(32)))
    lane8 = lax.broadcasted_iota(jnp.int32, (8, 128), 1)
    lower = lane8 < 64
    peak = jnp.max(logits, axis=0)
    neg = jnp.full((8, 128), -jnp.inf, F32)
    peak_low = jnp.max(jnp.where(lower, peak, neg), axis=1, keepdims=True)
    peak_high = jnp.max(jnp.where(lower, neg, peak), axis=1, keepdims=True)
    exponent = jnp.exp(logits - jnp.where(lower, peak_low, peak_high)[None])
    total = jnp.sum(exponent, axis=0)
    zero8 = jnp.zeros((8, 128), F32)
    total_low = jnp.sum(jnp.where(lower, total, zero8), axis=1, keepdims=True)
    total_high = jnp.sum(jnp.where(lower, zero8, total), axis=1, keepdims=True)
    weights = exponent / jnp.where(lower, total_low, total_high)[None]
    for z in range(4):
        even, odd = weights[2 * z], weights[2 * z + 1]
        wm[z] = jnp.where(lower, even, pltpu.roll(odd, 64, 1)).astype(BF16)
        wm[4 + z] = jnp.where(lower, pltpu.roll(even, 64, 1), odd).astype(BF16)

    seq_order = (7, 1, 2, 6, 3, 5, 4)
    keep = pltpu.make_async_copy(wm.at[:, 0:6], wg.at[s, :, 0:6], lsem.at[8])
    keep.start()
    for d in seq_order:
        send(wm.at[:, 0:6], wg.at[s, :, 0:6], ssem.at[15], rwg, (s + d) % 8, p)
    v_step(2, (2, 3))
    for n in range(36):
        w_pass(n)
    v_step(3, (0, 1, 2, 3))
    keep.wait()
    wait(wg.at[0:7, :, 0:6], rwg)
    wf[...] = wg[...].astype(F32)

    sums = wf[0]
    for i in range(1, 8):
        sums = sums + wf[i]
    base = c * 64 + y * 8
    for hh in range(2):
        placed = zero8
        for i in range(8):
            block = wf[i, hh * 4] + wf[i, hh * 4 + 1] + wf[i, hh * 4 + 2] + wf[i, hh * 4 + 3]
            placed = placed + jnp.where(
                lane8 == base + i, jnp.sum(block, axis=1, keepdims=True), zero8
            )
        for z in range(4):
            here = (zl == z).astype(F32)
            ptl[hh * 4 + z] = sums[hh * 4 + z] + here * placed
    ptz[zc] = ptl[s]
    for d in range(1, 8):
        send(ptl.at[s], ptz.at[zc], ssem.at[16], rpz, s, y * 8 + (zc + d) % 8)

    loads[8].wait()
    for z in range(4):
        acc = zero8
        for k in range(6):
            for hh in range(2):
                acc = acc + factor_ref[2 * k + hh] * wf[:, hh * 4 + z, k, :]
        mloc[z] = acc

    @pl.when(y == s)
    def _():
        for d in y_order:
            send(mloc, mrow, ssem.at[17], rm1, s, ((y + d) % 8) * 8 + zc)

    for at in range(4):
        wait(vg.at[0, 0, 0], rvr.at[at // 2, 3, (zl + v_order[at]) % 4])
    opposite = (y + 4) % 8
    v_sib(opposite)
    wait(vg.at[0], rvs)

    lower16 = lax.broadcasted_iota(jnp.int32, (8, 512), 1) % 128 < 64
    mixed = []
    for k in range(6):
        left = jnp.concatenate(
            [
                jnp.concatenate([wf[:, hh * 4 + z, k, :] for z in range(4)], axis=1)
                for hh in range(2)
            ],
            axis=0,
        ).astype(BF16)
        right = jnp.concatenate(
            [
                jnp.concatenate(
                    [vg[:, :, z, r, k].reshape(128, 128) for z in range(4)], axis=0
                )
                for r in range(4)
            ],
            axis=1,
        )
        both = jnp.dot(left, right, preferred_element_type=F32)
        mixed.append(jnp.where(lower16, both[0:8], both[8:16]))
    row_out = jnp.concatenate(
        [
            jnp.concatenate([mixed[k][:, r * 128 : r * 128 + 128] for k in range(6)], axis=1)
            for r in range(4)
        ],
        axis=0,
    ).astype(BF16)
    loads[4].wait()
    loads[6].wait()
    loads[7].wait()
    skip = jnp.concatenate(
        [
            jnp.concatenate([sk[r, k].astype(F32) for k in range(6)], axis=1)
            for r in range(4)
        ],
        axis=0,
    )
    scaling = jnp.concatenate([gain[k : k + 1, :] for k in range(6)], axis=1)
    hidden = skip + jnp.dot(row_out, wc[...], preferred_element_type=F32)
    hid[...] = hidden
    average = jnp.mean(hidden, axis=1, keepdims=True)
    centered = hidden - average
    spread = jnp.mean(centered * centered, axis=1, keepdims=True)
    normed = centered * lax.rsqrt(spread + 1e-05) * scaling
    for r in range(4):
        for k in range(6):
            nf[:, r * 6 + k, :] = normed[r * 8 : r * 8 + 8, k * 128 : k * 128 + 128]
    nm[:, 0] = nf[0:4].astype(BF16)
    nm[:, 1] = nf[4:8].astype(BF16)
    keep = pltpu.make_async_copy(nm.at[x], ng.at[s], lsem.at[9])
    keep.start()
    for d in seq_order:
        send(nm.at[((s + d) % 8) // 2], ng.at[s], ssem.at[18], rng, (s + d) % 8, p)

    for n in range(36):
        w_last(n)
    wait(ptz.at[0:7], rpz)
    acc = ptz[0]
    for z in range(1, 8):
        acc = acc + ptz[z]
    stage[0] = acc
    pty[y] = acc
    for d in y_order:
        send(stage.at[0], pty.at[y], ssem.at[19], rpy, s, ((y + d) % 8) * 8 + zc)
    for u in range(9):
        group, index, src, dst = w_unit(u)

        @pl.when(group == zh)
        def _():
            pltpu.make_async_copy(src, dst, wlocal.at[u]).wait()

    wait(wb.at[0:576, :], rww)

    wait(pty.at[0:7], rpy)
    acc = pty[0]
    for o in range(1, 8):
        acc = acc + pty[o]
    stage[1] = acc
    pts[s] = acc
    for d in seq_order:
        send(stage.at[1], pts.at[s], ssem.at[21], rps, (s + d) % 8, p)

    @pl.when(y == s)
    def _():
        mrow[...] = mloc[...]

    @pl.when(y != s)
    def _():
        wait(mrow, rm1)

    mcol[zc] = mrow[zl]
    for d in range(1, 8):
        o = (zc + d) % 8
        send(mrow.at[o // 2], mcol.at[zc], ssem.at[22], rm2, s, y * 8 + o)

    keep.wait()
    wait(ng.at[0:7], rng)
    gf[...] = ng[...].astype(F32)
    cells = jnp.concatenate(
        [
            jnp.concatenate([gf[:, b, r * 6 + k, :] for k in range(6)], axis=1)
            for r in range(4)
            for b in range(2)
        ],
        axis=0,
    ).astype(BF16)
    proj[...] = lax.dot_general(cells, wb[...], NT, preferred_element_type=F32).astype(BF16)
    lane_low = lax.broadcasted_iota(jnp.int32, (64, 128), 1) < 64
    same = (
        lax.broadcasted_iota(jnp.int32, (128, 64), 0) // 8 % 2
        == lax.broadcasted_iota(jnp.int32, (128, 64), 1) // 8 % 2
    )
    for k in range(3):
        cq = proj[:, k * 128 : k * 128 + 128]
        ck = proj[:, 384 + k * 128 : 384 + k * 128 + 128]
        cv = proj[:, 768 + k * 128 : 768 + k * 128 + 128]
        left = jnp.concatenate(
            [jnp.where(lane_low, cq, zero64), jnp.where(lane_low, zero64, cq)], axis=0
        )
        score = lax.dot_general(left, ck, NT, preferred_element_type=F32) * (1.0 / math.sqrt(64))
        exponent = jnp.where(same, jnp.exp(score), 0.0)
        share = (exponent / jnp.sum(exponent, axis=1, keepdims=True)).astype(BF16)
        both = jnp.dot(share, cv, preferred_element_type=F32)
        mix = jnp.where(lane_low, both[0:64], both[64:128])
        for r in range(4):
            for b in range(2):
                nf[:, b * 12 + r * 3 + k, :] = mix[r * 16 + b * 8 : r * 16 + b * 8 + 8]
    cm[...] = nf[...].astype(BF16)
    keep = pltpu.make_async_copy(cm.at[s], cg.at[zh, x], lsem.at[10])
    keep.start()
    for d in seq_order:
        send(cm.at[(s + d) % 8], cg.at[zh, x], ssem.at[20], rcg, (s + d) % 8, p)

    wait(pts.at[0:7], rps)
    wait(mcol.at[0:7], rm2)
    row8 = lax.broadcasted_iota(jnp.int32, (8, 128), 0)
    scaled, cols = [], []
    for hh in range(2):
        whole = pts[hh * 4] + pts[hh * 4 + 1] + pts[hh * 4 + 2] + pts[hh * 4 + 3]
        head_total = jnp.where(row8 < 6, jnp.sum(whole, axis=1, keepdims=True), 1.0)
        factor = zero8
        for k in range(6):
            factor = jnp.where(row8 == k, factor_ref[2 * k + hh], factor)
        scaled.append(factor / head_total * pts[hh * 4 + zl])
    block = jnp.zeros((24, 64), F32)
    lane_at = lax.broadcasted_iota(jnp.int32, (128, 64), 0)
    col_at = lax.broadcasted_iota(jnp.int32, (128, 64), 1)
    wanted = ((col_at // 8) % 2) * 64 + s * 8 + col_at % 8
    for z in range(4):
        pick = jnp.where((lane_at == wanted) & (col_at // 16 == z), 1.0, 0.0).astype(F32)
        block = block + jnp.dot(
            jnp.concatenate([pts[z], pts[4 + z], mloc[z]], axis=0), pick,
            precision=HI, preferred_element_type=F32,
        )
    mine = jnp.where(lane8 == base + row8, 1.0, 0.0).astype(F32)
    rows_here = lax.dot_general(
        mine, jnp.concatenate(scaled, axis=0), NT, precision=HI, preferred_element_type=F32
    )
    product = jnp.dot(rows_here, block[0:16], precision=HI, preferred_element_type=F32)
    mirrored = lax.dot_general(
        mine, mcol[...].reshape(64, 128), NT, precision=HI, preferred_element_type=F32
    )
    pair_ref[...] = jax.nn.sigmoid(block[16:24] + mirrored - product + offset_ref[0])

    wait(qg.at[0:4], ssem.at[0])
    wait(qg.at[0:3], ssem.at[1])
    wait(kg.at[0:7], ssem.at[2])
    wait(vg.at[0, 0, 0:3], ssem.at[3])
    for u in range(9):
        group = w_unit(u)[0]

        @pl.when(group == zh)
        def _():
            wait(wb.at[0:64, :], wsu.at[u])

        @pl.when(group != zh)
        def _():
            wait(wb.at[0:16, :], wsu.at[u])

    for n in range(36):
        lands, mine, dst = w_place(n)

        @pl.when(lands)
        def _():
            wait(wb.at[0:48, :], wsf.at[n])

        @pl.when(jnp.logical_not(mine))
        def _():
            wait(wb.at[0:16, :], wss.at[n])

    wait(rs.at[0:63, 0:6], ssem.at[11])
    wait(vg.at[0, 0:7], ssem.at[13])
    wait(vg.at[0], ssem.at[14])
    wait(wg.at[0:7, :, 0:6], ssem.at[15])
    wait(ptz.at[0:7], ssem.at[16])

    @pl.when(y == s)
    def _():
        wait(rs.at[0:28], ssem.at[17])

    wait(ng.at[0:7], ssem.at[18])
    wait(pty.at[0:7], ssem.at[19])
    wait(pts.at[0:7], ssem.at[21])
    wait(mcol.at[0:7], ssem.at[22])

    loads[5].wait()
    keep.wait()
    wait(cm.at[0:7], rcg)
    cf[...] = cg[...].astype(F32)
    cells = jnp.concatenate(
        [
            jnp.concatenate(
                [
                    jnp.concatenate(
                        [cf[k % 2, :, b * 12 + r * 3 + k // 2, :] for b in range(2)], axis=0
                    )
                    for k in range(6)
                ],
                axis=1,
            )
            for r in range(4)
        ],
        axis=0,
    ).astype(BF16)
    closing = hid[...] + jnp.dot(cells, wo[...], preferred_element_type=F32)
    for r in range(4):
        for k in range(6):
            out_ref[r, k] = closing[r * 8 : r * 8 + 8, k * 128 : k * 128 + 128].astype(BF16)

    wait(cm.at[0:7], ssem.at[20])


def per_device(
    skip_stream_input,
    lateral_asking_vectors,
    lateral_matched_vectors,
    lateral_carried_vectors,
    lateral_closing_linear,
    upright_normalizer_multiplier,
    upright_threefold_linear,
    upright_closing_linear,
    regression_factors,
    regression_offset,
):
    def tiles(array):
        return array.reshape(4, 8, 6, 128).transpose(0, 2, 1, 3)

    def vmem(*shape, dtype=BF16):
        return pltpu.VMEM(shape, dtype)

    def dma(*shape):
        return pltpu.SemaphoreType.DMA(shape)

    anywhere = pl.BlockSpec(memory_space=pltpu.HBM)
    in_vmem = pl.BlockSpec(memory_space=pltpu.VMEM)
    one = pltpu.SemaphoreType.DMA
    aligned, pairs = pl.pallas_call(
        body,
        out_shape=(
            pltpu.VMEM((4, 6, 8, 128), BF16),
            pltpu.VMEM((8, 64), F32),
        ),
        in_specs=[anywhere] * 9 + [pl.BlockSpec(memory_space=pltpu.SMEM)],
        out_specs=(in_vmem, in_vmem),
        scratch_shapes=[
            vmem(8, 4, 6, 8, 128),
            vmem(8, 4, 6, 8, 128),
            vmem(2, 8, 4, 4, 6, 8, 128),
            vmem(1152, 768),
            vmem(768, 768),
            vmem(768, 768),
            vmem(4, 6, 8, 128),
            vmem(64, 8, 128, dtype=F32),
            vmem(64, 8, 128, dtype=F32),
            vmem(8, 8, 128),
            vmem(8, 8, 8, 128),
            vmem(8, 8, 8, 128, dtype=F32),
            vmem(8, 24, 128, dtype=F32),
            vmem(4, 2, 24, 128),
            vmem(8, 2, 24, 128),
            vmem(8, 24, 128),
            vmem(2, 4, 24, 128),
            vmem(8, 2, 24, 128, dtype=F32),
            vmem(2, 4, 24, 128, dtype=F32),
            vmem(32, 768, dtype=F32),
            vmem(64, 1152),
            vmem(6, 128, dtype=F32),
            pltpu.SMEM((12,), F32),
            vmem(8, 8, 128, dtype=F32),
            vmem(8, 8, 128, dtype=F32),
            vmem(8, 8, 128, dtype=F32),
            vmem(8, 8, 128, dtype=F32),
            vmem(4, 8, 128, dtype=F32),
            vmem(4, 8, 128, dtype=F32),
            vmem(8, 8, 128, dtype=F32),
            vmem(2, 8, 128, dtype=F32),
            dma(14),
            dma(23),
            dma(4),
            dma(4),
            one,
            dma(4),
            one,
            dma(2, 4, 4),
            dma(36),
            one,
            dma(9),
            dma(9),
            dma(36),
            dma(36),
            one,
            one,
            one,
            one,
            one,
            one,
            one,
            one,
            one,
        ],
        compiler_params=pltpu.CompilerParams(
            collective_id=0, has_side_effects=True, vmem_limit_bytes=62 << 20
        ),
        name="axial_layer",
    )(
        tiles(skip_stream_input),
        tiles(lateral_asking_vectors),
        tiles(lateral_matched_vectors),
        tiles(lateral_carried_vectors),
        lateral_closing_linear,
        upright_normalizer_multiplier.reshape(6, 128),
        upright_threefold_linear.T,
        upright_closing_linear,
        regression_factors,
        regression_offset,
    )
    return aligned.transpose(0, 2, 1, 3).reshape(4, 8, 768), pairs


def solution(mesh):
    placed = (
        P("seq", "pos", None),
        P("seq", "pos", None),
        P("seq", "pos", None),
        P("seq", "pos", None),
        P(),
        P(),
        P(None, "seq"),
        P(),
        P(),
        P(),
    )
    return jax.shard_map(
        per_device,
        mesh=mesh,
        in_specs=placed,
        out_specs=(P("seq", "pos", None), P("pos", "seq")),
        check_vma=False,
    )
```

```python
import math

import jax
import jax.numpy as jnp
from jax import lax
from jax.experimental import pallas as pl
from jax.experimental.pallas import tpu as pltpu
from jax.sharding import PartitionSpec as P

MESH = pl.DeviceIdType.MESH
HI = lax.Precision.HIGHEST
F32 = jnp.float32
BF16 = jnp.bfloat16
NT = (((1,), (1,)), ((), ()))


def body(
    skip_hbm, q_hbm, k_hbm, v_hbm, wc_hbm, gain_hbm, w3_hbm, wo_hbm, factor_hbm, offset_ref,
    out_ref, pair_ref,
    qg, kg, vg, wb, wc, wo, sk,
    part, rs, wm, wg, wf, nf, nm, ng, cm, cg, gf, cf, hid, proj, gain, factor_ref,
    ptl, ptz, pty, pts, mloc, mrow, mcol, stage,
    lsem, ssem, rq, rqs, rk, rva, rvs, rvr, rw, rww, wlocal, wsu, wsf, wss, rrs, rwg, rng, rcg, rpz, rpy, rps, rm1, rm2,
):
    s = lax.axis_index("seq")
    p = lax.axis_index("pos")
    x, zh = s // 2, s % 2
    y, zc = p // 8, p % 8
    zl, c = zc // 2, zc % 2
    sib = y * 8 + zl * 2 + (1 - c)

    def local(src, dst, index):
        copy = pltpu.make_async_copy(src, dst, lsem.at[index])
        copy.start()
        return copy

    def send(src, dst, send_sem, recv_sem, seq, pos):
        pltpu.make_async_remote_copy(
            src_ref=src, dst_ref=dst, send_sem=send_sem, recv_sem=recv_sem,
            device_id=(seq, pos), device_id_type=MESH,
        ).start()

    def wait(ref, sem):
        pltpu.make_async_copy(ref, ref, sem).wait()

    barrier = pltpu.get_barrier_semaphore()
    plane = s * 8 + zc
    for d in (4, 3, 5, 2, 6, 1, 7):
        for peer in (((s + d) % 8, p), (s, ((y + d) % 8) * 8 + zc), (s, y * 8 + (zc + d) % 8)):
            pl.semaphore_signal(barrier, inc=1, device_id=peer, device_id_type=MESH)
    loads = [
        local(q_hbm, qg.at[zc], 0),
        local(k_hbm, kg.at[y], 1),
        local(v_hbm, vg.at[c, y, zl], 2),
        None,
        local(wc_hbm, wc, 4),
        local(wo_hbm, wo, 5),
        local(skip_hbm, sk, 6),
        local(gain_hbm, gain, 11),
        local(factor_hbm, factor_ref, 12),
    ]
    pl.semaphore_wait(barrier, 21)

    y_order = (4, 3, 5, 2, 6, 1, 7)
    up, down = ((y + 1) % 8) * 8 + zc, ((y + 7) % 8) * 8 + zc
    z_order = (2, 1, 3)
    for d in z_order:
        send(q_hbm, qg.at[zc], ssem.at[1], rq.at[zl], s, y * 8 + ((zl + d) % 4) * 2 + c)
    send(q_hbm, qg.at[zc], ssem.at[0], rqs.at[zl], s, sib)
    for d in z_order:
        send(v_hbm, vg.at[c, y, zl], ssem.at[3], rva.at[zl], s, y * 8 + ((zl + d) % 4) * 2 + c)
    for d in y_order:
        send(k_hbm, kg.at[y], ssem.at[2], rk, s, ((y + d) % 8) * 8 + zc)

    def x_peers(src, dst, send_sem, recv_sem):
        for d in (2, 1, 3):
            send(src, dst, send_sem, recv_sem, ((x + d) % 4) * 2 + zh, p)

    def w_unit(u, shard=s):
        col = shard * 288 + 32 * u
        role, within = col // 768, col % 768
        pair = within // 128
        index = role * 12 + (pair // 2) * 4 + (within % 128) // 32
        src = w3_hbm.at[pl.ds(pl.multiple_of(32 * u + c * 16, 16), 16), :]
        dst = wb.at[pl.ds(pl.multiple_of(index * 32 + c * 16, 16), 16), :]
        return pair % 2, index, src, dst

    def w_near(u):
        group, index, src, dst = w_unit(u)

        @pl.when(group == zh)
        def _():
            pltpu.make_async_copy(src, dst, wlocal.at[u]).start()
            x_peers(src, dst, wsu.at[u], rw.at[index])
            send(src, dst, wsu.at[u], rww, s, sib)

    def w_far(u):
        group, index, src, dst = w_unit(u)

        @pl.when(group != zh)
        def _():
            send(src, dst, wsu.at[u], rw.at[index], x * 2 + 1 - zh, p)

    def w_place(n):
        col = (n // 12) * 768 + (n % 12 // 4) * 256 + zh * 128 + (n % 4) * 32
        owner = col // 288
        here = owner // 2 == x
        far = owner % 2 != zh
        return far & here, jnp.logical_not(far) & here, wb.at[pl.ds(pl.multiple_of(n * 32 + c * 16, 16), 16), :]

    def w_pass(u):
        group, index, src, dst = w_unit(u, x * 2 + 1 - zh)

        @pl.when(group == zh)
        def _():
            wait(dst, rw.at[index])
            x_peers(dst, dst, wsf.at[index], rw.at[index])
            send(dst, dst, wss.at[index], rww, s, sib)

    def w_last(n):
        lands, mine, dst = w_place(n)

        @pl.when(jnp.logical_not(lands | mine))
        def _():
            wait(dst, rw.at[n])
            send(dst, dst, wss.at[n], rww, s, sib)

    for u in range(9):
        w_near(u)

    rs[:, 6:8, :] = jnp.zeros((64, 2, 128), F32)
    wg[:, :, 6:8, :] = jnp.zeros((8, 8, 2, 128), BF16)

    def v_unit(block, unit, way, step, target):
        send(
            vg.at[c, block, unit], vg.at[c, block, unit], ssem.at[13], rvr.at[way, step, unit], s, target
        )

    def v_sib(block):
        send(vg.at[c, block], vg.at[c, block], ssem.at[14], rvs, s, sib)

    v_order = (0, 1, 3, 2)

    def v_step(step, places):
        below, above = (y + 8 - step) % 8, (y + step) % 8
        for at in places:
            unit = (zl + v_order[at]) % 4
            wait(vg.at[0, 0, 0], rvr.at[0, step - 1, unit])
            if step < 3 or at < 2:
                v_unit(below, unit, 0, step, up)
            wait(vg.at[0, 0, 0], rvr.at[1, step - 1, unit])
            if step < 3 or at >= 2:
                v_unit(above, unit, 1, step, down)
        if 3 in places:
            v_sib(below)
            v_sib(above)

    for d in (1, 3, 2):
        other = (zl + d) % 4
        wait(qg.at[0], rq.at[other])
        send(
            qg.at[other * 2 + c], qg.at[other * 2 + c], ssem.at[0], rqs.at[other], s, sib
        )
    loads[0].wait()
    loads[1].wait()
    for other in range(4):
        wait(qg.at[0], rqs.at[other])
    send(v_hbm, vg.at[c, y, zl], ssem.at[13], rvr.at[0, 0, zl], s, up)
    send(v_hbm, vg.at[c, y, zl], ssem.at[13], rvr.at[1, 0, zl], s, down)
    for u in range(9):
        w_far(u)
    wait(kg.at[0:7], rk)

    loads[2].wait()
    for d in (1, 3, 2):
        other = (zl + d) % 4
        wait(vg.at[0, 0, 0], rva.at[other])
        v_unit(y, other, 0, 0, up)
        v_unit(y, other, 1, 0, down)
    v_sib(y)
    lane64 = lax.broadcasted_iota(jnp.int32, (64, 128), 1) < 64
    zero64 = jnp.zeros((64, 128), BF16)
    for k in range(6):
        left = jnp.concatenate([qg[:, r, k].reshape(64, 128) for r in range(4)], axis=1)
        keys = [kg[:, r, k].reshape(64, 128) for r in range(4)]
        low = jnp.concatenate([jnp.where(lane64, b, zero64) for b in keys], axis=1)
        high = jnp.concatenate([jnp.where(lane64, zero64, b) for b in keys], axis=1)
        tile = lax.dot_general(
            left, jnp.concatenate([low, high], axis=0), NT, preferred_element_type=F32
        )
        part[:, k, :] = tile

    own = pltpu.make_async_copy(part.at[zc * 8 + s, 0:6], rs.at[plane, 0:6], lsem.at[7])
    own.start()

    for d in range(1, 64):
        so, zo = (s + d // 8) % 8, (zc + d % 8) % 8
        send(part.at[zo * 8 + so, 0:6], rs.at[plane, 0:6], ssem.at[11], rrs, so, y * 8 + zo)

    v_step(1, (0, 1, 2, 3))
    v_step(2, (0, 1, 2))
    own.wait()
    wait(rs.at[0:63, 0:6], rrs)
    logits = rs[0:8]
    for so in range(1, 8):
        logits = logits + rs[so * 8 : so * 8 + 8]
    logits = logits * (1.0 / (math.sqrt(64) * math.sqrt(32)))
    lane8 = lax.broadcasted_iota(jnp.int32, (8, 128), 1)
    lower = lane8 < 64
    peak = jnp.max(logits, axis=0)
    neg = jnp.full((8, 128), -jnp.inf, F32)
    peak_low = jnp.max(jnp.where(lower, peak, neg), axis=1, keepdims=True)
    peak_high = jnp.max(jnp.where(lower, neg, peak), axis=1, keepdims=True)
    exponent = jnp.exp(logits - jnp.where(lower, peak_low, peak_high)[None])
    total = jnp.sum(exponent, axis=0)
    zero8 = jnp.zeros((8, 128), F32)
    total_low = jnp.sum(jnp.where(lower, total, zero8), axis=1, keepdims=True)
    total_high = jnp.sum(jnp.where(lower, zero8, total), axis=1, keepdims=True)
    weights = exponent / jnp.where(lower, total_low, total_high)[None]
    for z in range(4):
        even, odd = weights[2 * z], weights[2 * z + 1]
        wm[z] = jnp.where(lower, even, pltpu.roll(odd, 64, 1)).astype(BF16)
        wm[4 + z] = jnp.where(lower, pltpu.roll(even, 64, 1), odd).astype(BF16)

    seq_order = (7, 1, 2, 6, 3, 5, 4)
    keep = pltpu.make_async_copy(wm.at[:, 0:6], wg.at[s, :, 0:6], lsem.at[8])
    keep.start()
    for d in seq_order:
        send(wm.at[:, 0:6], wg.at[s, :, 0:6], ssem.at[15], rwg, (s + d) % 8, p)
    v_step(2, (3,))
    for u in range(9):
        w_pass(u)
    v_step(3, (0, 1, 2, 3))
    keep.wait()
    wait(wg.at[0:7, :, 0:6], rwg)
    wf[...] = wg[...].astype(F32)

    sums = wf[0]
    for i in range(1, 8):
        sums = sums + wf[i]
    base = c * 64 + y * 8
    for hh in range(2):
        placed = zero8
        for i in range(8):
            block = wf[i, hh * 4] + wf[i, hh * 4 + 1] + wf[i, hh * 4 + 2] + wf[i, hh * 4 + 3]
            placed = placed + jnp.where(
                lane8 == base + i, jnp.sum(block, axis=1, keepdims=True), zero8
            )
        for z in range(4):
            here = (zl == z).astype(F32)
            ptl[hh * 4 + z] = sums[hh * 4 + z] + here * placed
    ptz[zc] = ptl[s]
    for d in range(1, 8):
        send(ptl.at[s], ptz.at[zc], ssem.at[16], rpz, s, y * 8 + (zc + d) % 8)

    loads[8].wait()
    for z in range(4):
        acc = zero8
        for k in range(6):
            for hh in range(2):
                acc = acc + factor_ref[2 * k + hh] * wf[:, hh * 4 + z, k, :]
        mloc[z] = acc

    @pl.when(y == s)
    def _():
        for d in y_order:
            send(mloc, mrow, ssem.at[17], rm1, s, ((y + d) % 8) * 8 + zc)

    opposite = (y + 4) % 8
    for at in (0, 3, 1, 2):
        unit = (zl + v_order[at]) % 4
        wait(vg.at[0, 0, 0], rvr.at[at // 2, 3, unit])
        send(vg.at[c, opposite, unit], vg.at[c, opposite, unit], ssem.at[14], rvs, s, sib)
    wait(vg.at[0], rvs)

    lower16 = lax.broadcasted_iota(jnp.int32, (8, 512), 1) % 128 < 64
    mixed = []
    for k in range(6):
        left = jnp.concatenate(
            [
                jnp.concatenate([wf[:, hh * 4 + z, k, :] for z in range(4)], axis=1)
                for hh in range(2)
            ],
            axis=0,
        ).astype(BF16)
        right = jnp.concatenate(
            [
                jnp.concatenate(
                    [vg[:, :, z, r, k].reshape(128, 128) for z in range(4)], axis=0
                )
                for r in range(4)
            ],
            axis=1,
        )
        both = jnp.dot(left, right, preferred_element_type=F32)
        mixed.append(jnp.where(lower16, both[0:8], both[8:16]))
    row_out = jnp.concatenate(
        [
            jnp.concatenate([mixed[k][:, r * 128 : r * 128 + 128] for k in range(6)], axis=1)
            for r in range(4)
        ],
        axis=0,
    ).astype(BF16)
    loads[4].wait()
    loads[6].wait()
    loads[7].wait()
    skip = jnp.concatenate(
        [
            jnp.concatenate([sk[r, k].astype(F32) for k in range(6)], axis=1)
            for r in range(4)
        ],
        axis=0,
    )
    scaling = jnp.concatenate([gain[k : k + 1, :] for k in range(6)], axis=1)
    hidden = skip + jnp.dot(row_out, wc[...], preferred_element_type=F32)
    hid[...] = hidden
    average = jnp.mean(hidden, axis=1, keepdims=True)
    centered = hidden - average
    spread = jnp.mean(centered * centered, axis=1, keepdims=True)
    normed = centered * lax.rsqrt(spread + 1e-05) * scaling
    for r in range(4):
        for k in range(6):
            nf[:, r * 6 + k, :] = normed[r * 8 : r * 8 + 8, k * 128 : k * 128 + 128]
    nm[:, 0] = nf[0:4].astype(BF16)
    nm[:, 1] = nf[4:8].astype(BF16)
    keep = pltpu.make_async_copy(nm.at[x], ng.at[s], lsem.at[9])
    keep.start()
    for d in seq_order:
        send(nm.at[((s + d) % 8) // 2], ng.at[s], ssem.at[18], rng, (s + d) % 8, p)

    for n in range(36):
        w_last(n)
    wait(ptz.at[0:7], rpz)
    acc = ptz[0]
    for z in range(1, 8):
        acc = acc + ptz[z]
    stage[0] = acc
    pty[y] = acc
    for d in y_order:
        send(stage.at[0], pty.at[y], ssem.at[19], rpy, s, ((y + d) % 8) * 8 + zc)
    for u in range(9):
        group, index, src, dst = w_unit(u)

        @pl.when(group == zh)
        def _():
            pltpu.make_async_copy(src, dst, wlocal.at[u]).wait()

    wait(wb.at[0:576, :], rww)

    wait(pty.at[0:7], rpy)
    acc = pty[0]
    for o in range(1, 8):
        acc = acc + pty[o]
    stage[1] = acc
    pts[s] = acc
    for d in seq_order:
        send(stage.at[1], pts.at[s], ssem.at[21], rps, (s + d) % 8, p)

    @pl.when(y == s)
    def _():
        mrow[...] = mloc[...]

    @pl.when(y != s)
    def _():
        wait(mrow, rm1)

    mcol[zc] = mrow[zl]
    for d in range(1, 8):
        o = (zc + d) % 8
        send(mrow.at[o // 2], mcol.at[zc], ssem.at[22], rm2, s, y * 8 + o)

    keep.wait()
    wait(ng.at[0:7], rng)
    gf[...] = ng[...].astype(F32)
    cells = jnp.concatenate(
        [
            jnp.concatenate([gf[:, b, r * 6 + k, :] for k in range(6)], axis=1)
            for r in range(4)
            for b in range(2)
        ],
        axis=0,
    ).astype(BF16)
    proj[...] = lax.dot_general(cells, wb[...], NT, preferred_element_type=F32).astype(BF16)
    lane_low = lax.broadcasted_iota(jnp.int32, (64, 128), 1) < 64
    same = (
        lax.broadcasted_iota(jnp.int32, (128, 64), 0) // 8 % 2
        == lax.broadcasted_iota(jnp.int32, (128, 64), 1) // 8 % 2
    )
    for k in range(3):
        cq = proj[:, k * 128 : k * 128 + 128]
        ck = proj[:, 384 + k * 128 : 384 + k * 128 + 128]
        cv = proj[:, 768 + k * 128 : 768 + k * 128 + 128]
        left = jnp.concatenate(
            [jnp.where(lane_low, cq, zero64), jnp.where(lane_low, zero64, cq)], axis=0
        )
        score = lax.dot_general(left, ck, NT, preferred_element_type=F32) * (1.0 / math.sqrt(64))
        exponent = jnp.where(same, jnp.exp(score), 0.0)
        share = (exponent / jnp.sum(exponent, axis=1, keepdims=True)).astype(BF16)
        both = jnp.dot(share, cv, preferred_element_type=F32)
        mix = jnp.where(lane_low, both[0:64], both[64:128])
        for r in range(4):
            for b in range(2):
                nf[:, b * 12 + r * 3 + k, :] = mix[r * 16 + b * 8 : r * 16 + b * 8 + 8]
    cm[...] = nf[...].astype(BF16)
    keep = pltpu.make_async_copy(cm.at[s], cg.at[zh, x], lsem.at[10])
    keep.start()
    for d in seq_order:
        send(cm.at[(s + d) % 8], cg.at[zh, x], ssem.at[20], rcg, (s + d) % 8, p)

    wait(pts.at[0:7], rps)
    wait(mcol.at[0:7], rm2)
    row8 = lax.broadcasted_iota(jnp.int32, (8, 128), 0)
    scaled, cols = [], []
    for hh in range(2):
        whole = pts[hh * 4] + pts[hh * 4 + 1] + pts[hh * 4 + 2] + pts[hh * 4 + 3]
        head_total = jnp.where(row8 < 6, jnp.sum(whole, axis=1, keepdims=True), 1.0)
        factor = zero8
        for k in range(6):
            factor = jnp.where(row8 == k, factor_ref[2 * k + hh], factor)
        scaled.append(factor / head_total * pts[hh * 4 + zl])
    block = jnp.zeros((24, 64), F32)
    lane_at = lax.broadcasted_iota(jnp.int32, (128, 64), 0)
    col_at = lax.broadcasted_iota(jnp.int32, (128, 64), 1)
    wanted = ((col_at // 8) % 2) * 64 + s * 8 + col_at % 8
    for z in range(4):
        pick = jnp.where((lane_at == wanted) & (col_at // 16 == z), 1.0, 0.0).astype(F32)
        block = block + jnp.dot(
            jnp.concatenate([pts[z], pts[4 + z], mloc[z]], axis=0), pick,
            precision=HI, preferred_element_type=F32,
        )
    mine = jnp.where(lane8 == base + row8, 1.0, 0.0).astype(F32)
    rows_here = lax.dot_general(
        mine, jnp.concatenate(scaled, axis=0), NT, precision=HI, preferred_element_type=F32
    )
    product = jnp.dot(rows_here, block[0:16], precision=HI, preferred_element_type=F32)
    mirrored = lax.dot_general(
        mine, mcol[...].reshape(64, 128), NT, precision=HI, preferred_element_type=F32
    )
    pair_ref[...] = jax.nn.sigmoid(block[16:24] + mirrored - product + offset_ref[0])

    wait(qg.at[0:4], ssem.at[0])
    wait(qg.at[0:3], ssem.at[1])
    wait(kg.at[0:7], ssem.at[2])
    wait(vg.at[0, 0, 0:3], ssem.at[3])
    for u in range(9):
        group = w_unit(u)[0]

        @pl.when(group == zh)
        def _():
            wait(wb.at[0:64, :], wsu.at[u])

        @pl.when(group != zh)
        def _():
            wait(wb.at[0:16, :], wsu.at[u])

    for n in range(36):
        lands, mine, dst = w_place(n)

        @pl.when(lands)
        def _():
            wait(wb.at[0:48, :], wsf.at[n])

        @pl.when(jnp.logical_not(mine))
        def _():
            wait(wb.at[0:16, :], wss.at[n])

    wait(rs.at[0:63, 0:6], ssem.at[11])
    wait(vg.at[0, 0:7], ssem.at[13])
    wait(vg.at[0], ssem.at[14])
    wait(wg.at[0:7, :, 0:6], ssem.at[15])
    wait(ptz.at[0:7], ssem.at[16])

    @pl.when(y == s)
    def _():
        wait(rs.at[0:28], ssem.at[17])

    wait(ng.at[0:7], ssem.at[18])
    wait(pty.at[0:7], ssem.at[19])
    wait(pts.at[0:7], ssem.at[21])
    wait(mcol.at[0:7], ssem.at[22])

    loads[5].wait()
    keep.wait()
    wait(cm.at[0:7], rcg)
    cf[...] = cg[...].astype(F32)
    cells = jnp.concatenate(
        [
            jnp.concatenate(
                [
                    jnp.concatenate(
                        [cf[k % 2, :, b * 12 + r * 3 + k // 2, :] for b in range(2)], axis=0
                    )
                    for k in range(6)
                ],
                axis=1,
            )
            for r in range(4)
        ],
        axis=0,
    ).astype(BF16)
    closing = hid[...] + jnp.dot(cells, wo[...], preferred_element_type=F32)
    for r in range(4):
        for k in range(6):
            out_ref[r, k] = closing[r * 8 : r * 8 + 8, k * 128 : k * 128 + 128].astype(BF16)

    wait(cm.at[0:7], ssem.at[20])


def per_device(
    skip_stream_input,
    lateral_asking_vectors,
    lateral_matched_vectors,
    lateral_carried_vectors,
    lateral_closing_linear,
    upright_normalizer_multiplier,
    upright_threefold_linear,
    upright_closing_linear,
    regression_factors,
    regression_offset,
):
    def tiles(array):
        return array.reshape(4, 8, 6, 128).transpose(0, 2, 1, 3)

    def vmem(*shape, dtype=BF16):
        return pltpu.VMEM(shape, dtype)

    def dma(*shape):
        return pltpu.SemaphoreType.DMA(shape)

    anywhere = pl.BlockSpec(memory_space=pltpu.HBM)
    in_vmem = pl.BlockSpec(memory_space=pltpu.VMEM)
    one = pltpu.SemaphoreType.DMA
    aligned, pairs = pl.pallas_call(
        body,
        out_shape=(
            pltpu.VMEM((4, 6, 8, 128), BF16),
            pltpu.VMEM((8, 64), F32),
        ),
        in_specs=[anywhere] * 9 + [pl.BlockSpec(memory_space=pltpu.SMEM)],
        out_specs=(in_vmem, in_vmem),
        scratch_shapes=[
            vmem(8, 4, 6, 8, 128),
            vmem(8, 4, 6, 8, 128),
            vmem(2, 8, 4, 4, 6, 8, 128),
            vmem(1152, 768),
            vmem(768, 768),
            vmem(768, 768),
            vmem(4, 6, 8, 128),
            vmem(64, 8, 128, dtype=F32),
            vmem(64, 8, 128, dtype=F32),
            vmem(8, 8, 128),
            vmem(8, 8, 8, 128),
            vmem(8, 8, 8, 128, dtype=F32),
            vmem(8, 24, 128, dtype=F32),
            vmem(4, 2, 24, 128),
            vmem(8, 2, 24, 128),
            vmem(8, 24, 128),
            vmem(2, 4, 24, 128),
            vmem(8, 2, 24, 128, dtype=F32),
            vmem(2, 4, 24, 128, dtype=F32),
            vmem(32, 768, dtype=F32),
            vmem(64, 1152),
            vmem(6, 128, dtype=F32),
            pltpu.SMEM((12,), F32),
            vmem(8, 8, 128, dtype=F32),
            vmem(8, 8, 128, dtype=F32),
            vmem(8, 8, 128, dtype=F32),
            vmem(8, 8, 128, dtype=F32),
            vmem(4, 8, 128, dtype=F32),
            vmem(4, 8, 128, dtype=F32),
            vmem(8, 8, 128, dtype=F32),
            vmem(2, 8, 128, dtype=F32),
            dma(14),
            dma(23),
            dma(4),
            dma(4),
            one,
            dma(4),
            one,
            dma(2, 4, 4),
            dma(36),
            one,
            dma(9),
            dma(9),
            dma(36),
            dma(36),
            one,
            one,
            one,
            one,
            one,
            one,
            one,
            one,
            one,
        ],
        compiler_params=pltpu.CompilerParams(
            collective_id=0, has_side_effects=True, vmem_limit_bytes=62 << 20
        ),
        name="axial_layer",
    )(
        tiles(skip_stream_input),
        tiles(lateral_asking_vectors),
        tiles(lateral_matched_vectors),
        tiles(lateral_carried_vectors),
        lateral_closing_linear,
        upright_normalizer_multiplier.reshape(6, 128),
        upright_threefold_linear.T,
        upright_closing_linear,
        regression_factors,
        regression_offset,
    )
    return aligned.transpose(0, 2, 1, 3).reshape(4, 8, 768), pairs


def solution(mesh):
    placed = (
        P("seq", "pos", None),
        P("seq", "pos", None),
        P("seq", "pos", None),
        P("seq", "pos", None),
        P(),
        P(),
        P(None, "seq"),
        P(),
        P(),
        P(),
    )
    return jax.shard_map(
        per_device,
        mesh=mesh,
        in_specs=placed,
        out_specs=(P("seq", "pos", None), P("pos", "seq")),
        check_vma=False,
    )
```

```python
import math

import jax
import jax.numpy as jnp
from jax import lax
from jax.experimental import pallas as pl
from jax.experimental.pallas import tpu as pltpu
from jax.sharding import PartitionSpec as P

MESH = pl.DeviceIdType.MESH
HI = lax.Precision.HIGHEST
F32 = jnp.float32
BF16 = jnp.bfloat16
NT = (((1,), (1,)), ((), ()))


def body(
    skip_hbm, q_hbm, k_hbm, v_hbm, wc_hbm, gain_hbm, w3_hbm, wo_hbm, factor_hbm, offset_ref,
    out_ref, pair_ref,
    qg, kg, vg, wb, wc, wo, sk,
    part, rs, wm, wg, wf, nf, nm, ng, cm, cg, gf, cf, hid, proj, gain, factor_ref,
    ptl, ptz, pty, pts, mloc, mrow, mcol, stage,
    lsem, ssem, rq, rqs, rk, rva, rvs, rvr, rw, rww, wlocal, wsu, wsf, wss, rrs, rwg, rng, rcg, rpz, rpy, rps, rm1, rm2,
):
    s = lax.axis_index("seq")
    p = lax.axis_index("pos")
    x, zh = s // 2, s % 2
    y, zc = p // 8, p % 8
    zl, c = zc // 2, zc % 2
    sib = y * 8 + zl * 2 + (1 - c)

    def local(src, dst, index):
        copy = pltpu.make_async_copy(src, dst, lsem.at[index])
        copy.start()
        return copy

    def send(src, dst, send_sem, recv_sem, seq, pos):
        pltpu.make_async_remote_copy(
            src_ref=src, dst_ref=dst, send_sem=send_sem, recv_sem=recv_sem,
            device_id=(seq, pos), device_id_type=MESH,
        ).start()

    def wait(ref, sem):
        pltpu.make_async_copy(ref, ref, sem).wait()

    barrier = pltpu.get_barrier_semaphore()
    plane = s * 8 + zc
    for d in (4, 3, 5, 2, 6, 1, 7):
        for peer in (((s + d) % 8, p), (s, ((y + d) % 8) * 8 + zc), (s, y * 8 + (zc + d) % 8)):
            pl.semaphore_signal(barrier, inc=1, device_id=peer, device_id_type=MESH)
    loads = [
        local(q_hbm, qg.at[zc], 0),
        local(k_hbm, kg.at[y], 1),
        local(v_hbm, vg.at[c, y, zl], 2),
        None,
        local(wc_hbm, wc, 4),
        local(wo_hbm, wo, 5),
        local(skip_hbm, sk, 6),
        local(gain_hbm, gain, 11),
        local(factor_hbm, factor_ref, 12),
    ]
    pl.semaphore_wait(barrier, 21)

    y_order = (4, 3, 5, 2, 6, 1, 7)
    up, down = ((y + 1) % 8) * 8 + zc, ((y + 7) % 8) * 8 + zc
    z_order = (2, 1, 3)
    for d in z_order:
        send(q_hbm, qg.at[zc], ssem.at[1], rq.at[zl], s, y * 8 + ((zl + d) % 4) * 2 + c)
    send(q_hbm, qg.at[zc], ssem.at[0], rqs.at[zl], s, sib)
    for d in z_order:
        send(v_hbm, vg.at[c, y, zl], ssem.at[3], rva.at[zl], s, y * 8 + ((zl + d) % 4) * 2 + c)
    for d in y_order:
        send(k_hbm, kg.at[y], ssem.at[2], rk, s, ((y + d) % 8) * 8 + zc)

    def x_peers(src, dst, send_sem, recv_sem):
        for d in (2, 1, 3):
            send(src, dst, send_sem, recv_sem, ((x + d) % 4) * 2 + zh, p)

    def w_unit(u, shard=s):
        col = shard * 288 + 32 * u
        role, within = col // 768, col % 768
        pair = within // 128
        index = role * 12 + (pair // 2) * 4 + (within % 128) // 32
        src = w3_hbm.at[pl.ds(pl.multiple_of(32 * u + c * 16, 16), 16), :]
        dst = wb.at[pl.ds(pl.multiple_of(index * 32 + c * 16, 16), 16), :]
        return pair % 2, index, src, dst

    def w_near(u):
        group, index, src, dst = w_unit(u)

        @pl.when(group == zh)
        def _():
            pltpu.make_async_copy(src, dst, wlocal.at[u]).start()
            x_peers(src, dst, wsu.at[u], rw.at[index])
            send(src, dst, wsu.at[u], rww, s, sib)

    def w_far(u):
        group, index, src, dst = w_unit(u)

        @pl.when(group != zh)
        def _():
            send(src, dst, wsu.at[u], rw.at[index], x * 2 + 1 - zh, p)

    def w_place(n):
        col = (n // 12) * 768 + (n % 12 // 4) * 256 + zh * 128 + (n % 4) * 32
        owner = col // 288
        here = owner // 2 == x
        far = owner % 2 != zh
        return far & here, jnp.logical_not(far) & here, wb.at[pl.ds(pl.multiple_of(n * 32 + c * 16, 16), 16), :]

    def w_pass(u):
        group, index, src, dst = w_unit(u, x * 2 + 1 - zh)

        @pl.when(group == zh)
        def _():
            wait(dst, rw.at[index])
            x_peers(dst, dst, wsf.at[index], rw.at[index])
            send(dst, dst, wss.at[index], rww, s, sib)

    def w_last(n):
        lands, mine, dst = w_place(n)

        @pl.when(jnp.logical_not(lands | mine))
        def _():
            wait(dst, rw.at[n])
            send(dst, dst, wss.at[n], rww, s, sib)

    for u in range(9):
        w_near(u)

    rs[:, 6:8, :] = jnp.zeros((64, 2, 128), F32)
    wg[:, :, 6:8, :] = jnp.zeros((8, 8, 2, 128), BF16)

    def v_unit(block, unit, way, step, target):
        send(
            vg.at[c, block, unit], vg.at[c, block, unit], ssem.at[13], rvr.at[way, step, unit], s, target
        )

    def v_sib(block):
        send(vg.at[c, block], vg.at[c, block], ssem.at[14], rvs, s, sib)

    v_order = (0, 1, 3, 2)

    def v_step(step, places):
        below, above = (y + 8 - step) % 8, (y + step) % 8
        for at in places:
            unit = (zl + v_order[at]) % 4
            wait(vg.at[0, 0, 0], rvr.at[0, step - 1, unit])
            if step < 3 or at < 2:
                v_unit(below, unit, 0, step, up)
            wait(vg.at[0, 0, 0], rvr.at[1, step - 1, unit])
            if step < 3 or at >= 2:
                v_unit(above, unit, 1, step, down)
        if 3 in places:
            v_sib(below)
            v_sib(above)

    for d in (1, 3, 2):
        other = (zl + d) % 4
        wait(qg.at[0], rq.at[other])
        send(
            qg.at[other * 2 + c], qg.at[other * 2 + c], ssem.at[0], rqs.at[other], s, sib
        )
    loads[0].wait()
    loads[1].wait()
    for other in range(4):
        wait(qg.at[0], rqs.at[other])
    send(v_hbm, vg.at[c, y, zl], ssem.at[13], rvr.at[0, 0, zl], s, up)
    send(v_hbm, vg.at[c, y, zl], ssem.at[13], rvr.at[1, 0, zl], s, down)
    for u in range(9):
        w_far(u)
    wait(kg.at[0:7], rk)

    loads[2].wait()
    for d in (1, 3, 2):
        other = (zl + d) % 4
        wait(vg.at[0, 0, 0], rva.at[other])
        v_unit(y, other, 0, 0, up)
        v_unit(y, other, 1, 0, down)
    v_sib(y)
    lane64 = lax.broadcasted_iota(jnp.int32, (64, 128), 1) < 64
    zero64 = jnp.zeros((64, 128), BF16)
    for k in range(6):
        left = jnp.concatenate([qg[:, r, k].reshape(64, 128) for r in range(4)], axis=1)
        keys = [kg[:, r, k].reshape(64, 128) for r in range(4)]
        low = jnp.concatenate([jnp.where(lane64, b, zero64) for b in keys], axis=1)
        high = jnp.concatenate([jnp.where(lane64, zero64, b) for b in keys], axis=1)
        tile = lax.dot_general(
            left, jnp.concatenate([low, high], axis=0), NT, preferred_element_type=F32
        )
        part[:, k, :] = tile

    own = pltpu.make_async_copy(part.at[zc * 8 + s, 0:6], rs.at[plane, 0:6], lsem.at[7])
    own.start()

    for d in range(1, 64):
        so, zo = (s + d // 8) % 8, (zc + d % 8) % 8
        send(part.at[zo * 8 + so, 0:6], rs.at[plane, 0:6], ssem.at[11], rrs, so, y * 8 + zo)

    v_step(1, (0, 1, 2, 3))
    v_step(2, (0, 1, 2, 3))
    own.wait()
    wait(rs.at[0:63, 0:6], rrs)
    logits = rs[0:8]
    for so in range(1, 8):
        logits = logits + rs[so * 8 : so * 8 + 8]
    logits = logits * (1.0 / (math.sqrt(64) * math.sqrt(32)))
    lane8 = lax.broadcasted_iota(jnp.int32, (8, 128), 1)
    lower = lane8 < 64
    peak = jnp.max(logits, axis=0)
    neg = jnp.full((8, 128), -jnp.inf, F32)
    peak_low = jnp.max(jnp.where(lower, peak, neg), axis=1, keepdims=True)
    peak_high = jnp.max(jnp.where(lower, neg, peak), axis=1, keepdims=True)
    exponent = jnp.exp(logits - jnp.where(lower, peak_low, peak_high)[None])
    total = jnp.sum(exponent, axis=0)
    zero8 = jnp.zeros((8, 128), F32)
    total_low = jnp.sum(jnp.where(lower, total, zero8), axis=1, keepdims=True)
    total_high = jnp.sum(jnp.where(lower, zero8, total), axis=1, keepdims=True)
    weights = exponent / jnp.where(lower, total_low, total_high)[None]
    for z in range(4):
        even, odd = weights[2 * z], weights[2 * z + 1]
        wm[z] = jnp.where(lower, even, pltpu.roll(odd, 64, 1)).astype(BF16)
        wm[4 + z] = jnp.where(lower, pltpu.roll(even, 64, 1), odd).astype(BF16)

    seq_order = (7, 1, 2, 6, 3, 5, 4)
    keep = pltpu.make_async_copy(wm.at[:, 0:6], wg.at[s, :, 0:6], lsem.at[8])
    keep.start()
    for d in seq_order:
        send(wm.at[:, 0:6], wg.at[s, :, 0:6], ssem.at[15], rwg, (s + d) % 8, p)
    for u in range(9):
        w_pass(u)
    v_step(3, (0, 1, 2, 3))
    keep.wait()
    wait(wg.at[0:7, :, 0:6], rwg)
    wf[...] = wg[...].astype(F32)

    sums = wf[0]
    for i in range(1, 8):
        sums = sums + wf[i]
    base = c * 64 + y * 8
    for hh in range(2):
        placed = zero8
        for i in range(8):
            block = wf[i, hh * 4] + wf[i, hh * 4 + 1] + wf[i, hh * 4 + 2] + wf[i, hh * 4 + 3]
            placed = placed + jnp.where(
                lane8 == base + i, jnp.sum(block, axis=1, keepdims=True), zero8
            )
        for z in range(4):
            here = (zl == z).astype(F32)
            ptl[hh * 4 + z] = sums[hh * 4 + z] + here * placed
    ptz[zc] = ptl[s]
    for d in range(1, 8):
        send(ptl.at[s], ptz.at[zc], ssem.at[16], rpz, s, y * 8 + (zc + d) % 8)

    loads[8].wait()
    for z in range(4):
        acc = zero8
        for k in range(6):
            for hh in range(2):
                acc = acc + factor_ref[2 * k + hh] * wf[:, hh * 4 + z, k, :]
        mloc[z] = acc

    @pl.when(y == s)
    def _():
        for d in y_order:
            send(mloc, mrow, ssem.at[17], rm1, s, ((y + d) % 8) * 8 + zc)

    opposite = (y + 4) % 8
    for at in (0, 3, 1, 2):
        unit = (zl + v_order[at]) % 4
        wait(vg.at[0, 0, 0], rvr.at[at // 2, 3, unit])
        send(vg.at[c, opposite, unit], vg.at[c, opposite, unit], ssem.at[14], rvs, s, sib)
    wait(vg.at[0], rvs)

    lower16 = lax.broadcasted_iota(jnp.int32, (8, 512), 1) % 128 < 64
    mixed = []
    for k in range(6):
        left = jnp.concatenate(
            [
                jnp.concatenate([wf[:, hh * 4 + z, k, :] for z in range(4)], axis=1)
                for hh in range(2)
            ],
            axis=0,
        ).astype(BF16)
        right = jnp.concatenate(
            [
                jnp.concatenate(
                    [vg[:, :, z, r, k].reshape(128, 128) for z in range(4)], axis=0
                )
                for r in range(4)
            ],
            axis=1,
        )
        both = jnp.dot(left, right, preferred_element_type=F32)
        mixed.append(jnp.where(lower16, both[0:8], both[8:16]))
    row_out = jnp.concatenate(
        [
            jnp.concatenate([mixed[k][:, r * 128 : r * 128 + 128] for k in range(6)], axis=1)
            for r in range(4)
        ],
        axis=0,
    ).astype(BF16)
    loads[4].wait()
    loads[6].wait()
    loads[7].wait()
    skip = jnp.concatenate(
        [
            jnp.concatenate([sk[r, k].astype(F32) for k in range(6)], axis=1)
            for r in range(4)
        ],
        axis=0,
    )
    scaling = jnp.concatenate([gain[k : k + 1, :] for k in range(6)], axis=1)
    hidden = skip + jnp.dot(row_out, wc[...], preferred_element_type=F32)
    hid[...] = hidden
    average = jnp.mean(hidden, axis=1, keepdims=True)
    centered = hidden - average
    spread = jnp.mean(centered * centered, axis=1, keepdims=True)
    normed = centered * lax.rsqrt(spread + 1e-05) * scaling
    for r in range(4):
        for k in range(6):
            nf[:, r * 6 + k, :] = normed[r * 8 : r * 8 + 8, k * 128 : k * 128 + 128]
    nm[:, 0] = nf[0:4].astype(BF16)
    nm[:, 1] = nf[4:8].astype(BF16)
    keep = pltpu.make_async_copy(nm.at[x], ng.at[s], lsem.at[9])
    keep.start()
    for d in seq_order:
        send(nm.at[((s + d) % 8) // 2], ng.at[s], ssem.at[18], rng, (s + d) % 8, p)

    for n in range(36):
        w_last(n)
    wait(ptz.at[0:7], rpz)
    acc = ptz[0]
    for z in range(1, 8):
        acc = acc + ptz[z]
    stage[0] = acc
    pty[y] = acc
    for d in y_order:
        send(stage.at[0], pty.at[y], ssem.at[19], rpy, s, ((y + d) % 8) * 8 + zc)
    for u in range(9):
        group, index, src, dst = w_unit(u)

        @pl.when(group == zh)
        def _():
            pltpu.make_async_copy(src, dst, wlocal.at[u]).wait()

    wait(wb.at[0:576, :], rww)

    wait(pty.at[0:7], rpy)
    acc = pty[0]
    for o in range(1, 8):
        acc = acc + pty[o]
    stage[1] = acc
    pts[s] = acc
    for d in seq_order:
        send(stage.at[1], pts.at[s], ssem.at[21], rps, (s + d) % 8, p)

    @pl.when(y == s)
    def _():
        mrow[...] = mloc[...]

    @pl.when(y != s)
    def _():
        wait(mrow, rm1)

    mcol[zc] = mrow[zl]
    for d in range(1, 8):
        o = (zc + d) % 8
        send(mrow.at[o // 2], mcol.at[zc], ssem.at[22], rm2, s, y * 8 + o)

    keep.wait()
    wait(ng.at[0:7], rng)
    gf[...] = ng[...].astype(F32)
    cells = jnp.concatenate(
        [
            jnp.concatenate([gf[:, b, r * 6 + k, :] for k in range(6)], axis=1)
            for r in range(4)
            for b in range(2)
        ],
        axis=0,
    ).astype(BF16)
    proj[...] = lax.dot_general(cells, wb[...], NT, preferred_element_type=F32).astype(BF16)
    lane_low = lax.broadcasted_iota(jnp.int32, (64, 128), 1) < 64
    same = (
        lax.broadcasted_iota(jnp.int32, (128, 64), 0) // 8 % 2
        == lax.broadcasted_iota(jnp.int32, (128, 64), 1) // 8 % 2
    )
    for k in range(3):
        cq = proj[:, k * 128 : k * 128 + 128]
        ck = proj[:, 384 + k * 128 : 384 + k * 128 + 128]
        cv = proj[:, 768 + k * 128 : 768 + k * 128 + 128]
        left = jnp.concatenate(
            [jnp.where(lane_low, cq, zero64), jnp.where(lane_low, zero64, cq)], axis=0
        )
        score = lax.dot_general(left, ck, NT, preferred_element_type=F32) * (1.0 / math.sqrt(64))
        exponent = jnp.where(same, jnp.exp(score), 0.0)
        share = (exponent / jnp.sum(exponent, axis=1, keepdims=True)).astype(BF16)
        both = jnp.dot(share, cv, preferred_element_type=F32)
        mix = jnp.where(lane_low, both[0:64], both[64:128])
        for r in range(4):
            for b in range(2):
                nf[:, b * 12 + r * 3 + k, :] = mix[r * 16 + b * 8 : r * 16 + b * 8 + 8]
    cm[...] = nf[...].astype(BF16)
    keep = pltpu.make_async_copy(cm.at[s], cg.at[zh, x], lsem.at[10])
    keep.start()
    for d in seq_order:
        send(cm.at[(s + d) % 8], cg.at[zh, x], ssem.at[20], rcg, (s + d) % 8, p)

    wait(pts.at[0:7], rps)
    wait(mcol.at[0:7], rm2)
    row8 = lax.broadcasted_iota(jnp.int32, (8, 128), 0)
    scaled, cols = [], []
    for hh in range(2):
        whole = pts[hh * 4] + pts[hh * 4 + 1] + pts[hh * 4 + 2] + pts[hh * 4 + 3]
        head_total = jnp.where(row8 < 6, jnp.sum(whole, axis=1, keepdims=True), 1.0)
        factor = zero8
        for k in range(6):
            factor = jnp.where(row8 == k, factor_ref[2 * k + hh], factor)
        scaled.append(factor / head_total * pts[hh * 4 + zl])
    block = jnp.zeros((24, 64), F32)
    lane_at = lax.broadcasted_iota(jnp.int32, (128, 64), 0)
    col_at = lax.broadcasted_iota(jnp.int32, (128, 64), 1)
    wanted = ((col_at // 8) % 2) * 64 + s * 8 + col_at % 8
    for z in range(4):
        pick = jnp.where((lane_at == wanted) & (col_at // 16 == z), 1.0, 0.0).astype(F32)
        block = block + jnp.dot(
            jnp.concatenate([pts[z], pts[4 + z], mloc[z]], axis=0), pick,
            precision=HI, preferred_element_type=F32,
        )
    mine = jnp.where(lane8 == base + row8, 1.0, 0.0).astype(F32)
    rows_here = lax.dot_general(
        mine, jnp.concatenate(scaled, axis=0), NT, precision=HI, preferred_element_type=F32
    )
    product = jnp.dot(rows_here, block[0:16], precision=HI, preferred_element_type=F32)
    mirrored = lax.dot_general(
        mine, mcol[...].reshape(64, 128), NT, precision=HI, preferred_element_type=F32
    )
    pair_ref[...] = jax.nn.sigmoid(block[16:24] + mirrored - product + offset_ref[0])

    wait(qg.at[0:4], ssem.at[0])
    wait(qg.at[0:3], ssem.at[1])
    wait(kg.at[0:7], ssem.at[2])
    wait(vg.at[0, 0, 0:3], ssem.at[3])
    for u in range(9):
        group = w_unit(u)[0]

        @pl.when(group == zh)
        def _():
            wait(wb.at[0:64, :], wsu.at[u])

        @pl.when(group != zh)
        def _():
            wait(wb.at[0:16, :], wsu.at[u])

    for n in range(36):
        lands, mine, dst = w_place(n)

        @pl.when(lands)
        def _():
            wait(wb.at[0:48, :], wsf.at[n])

        @pl.when(jnp.logical_not(mine))
        def _():
            wait(wb.at[0:16, :], wss.at[n])

    wait(rs.at[0:63, 0:6], ssem.at[11])
    wait(vg.at[0, 0:7], ssem.at[13])
    wait(vg.at[0], ssem.at[14])
    wait(wg.at[0:7, :, 0:6], ssem.at[15])
    wait(ptz.at[0:7], ssem.at[16])

    @pl.when(y == s)
    def _():
        wait(rs.at[0:28], ssem.at[17])

    wait(ng.at[0:7], ssem.at[18])
    wait(pty.at[0:7], ssem.at[19])
    wait(pts.at[0:7], ssem.at[21])
    wait(mcol.at[0:7], ssem.at[22])

    loads[5].wait()
    keep.wait()
    wait(cm.at[0:7], rcg)
    cf[...] = cg[...].astype(F32)
    cells = jnp.concatenate(
        [
            jnp.concatenate(
                [
                    jnp.concatenate(
                        [cf[k % 2, :, b * 12 + r * 3 + k // 2, :] for b in range(2)], axis=0
                    )
                    for k in range(6)
                ],
                axis=1,
            )
            for r in range(4)
        ],
        axis=0,
    ).astype(BF16)
    closing = hid[...] + jnp.dot(cells, wo[...], preferred_element_type=F32)
    for r in range(4):
        for k in range(6):
            out_ref[r, k] = closing[r * 8 : r * 8 + 8, k * 128 : k * 128 + 128].astype(BF16)

    wait(cm.at[0:7], ssem.at[20])


def per_device(
    skip_stream_input,
    lateral_asking_vectors,
    lateral_matched_vectors,
    lateral_carried_vectors,
    lateral_closing_linear,
    upright_normalizer_multiplier,
    upright_threefold_linear,
    upright_closing_linear,
    regression_factors,
    regression_offset,
):
    def tiles(array):
        return array.reshape(4, 8, 6, 128).transpose(0, 2, 1, 3)

    def vmem(*shape, dtype=BF16):
        return pltpu.VMEM(shape, dtype)

    def dma(*shape):
        return pltpu.SemaphoreType.DMA(shape)

    anywhere = pl.BlockSpec(memory_space=pltpu.HBM)
    in_vmem = pl.BlockSpec(memory_space=pltpu.VMEM)
    one = pltpu.SemaphoreType.DMA
    aligned, pairs = pl.pallas_call(
        body,
        out_shape=(
            pltpu.VMEM((4, 6, 8, 128), BF16),
            pltpu.VMEM((8, 64), F32),
        ),
        in_specs=[anywhere] * 9 + [pl.BlockSpec(memory_space=pltpu.SMEM)],
        out_specs=(in_vmem, in_vmem),
        scratch_shapes=[
            vmem(8, 4, 6, 8, 128),
            vmem(8, 4, 6, 8, 128),
            vmem(2, 8, 4, 4, 6, 8, 128),
            vmem(1152, 768),
            vmem(768, 768),
            vmem(768, 768),
            vmem(4, 6, 8, 128),
            vmem(64, 8, 128, dtype=F32),
            vmem(64, 8, 128, dtype=F32),
            vmem(8, 8, 128),
            vmem(8, 8, 8, 128),
            vmem(8, 8, 8, 128, dtype=F32),
            vmem(8, 24, 128, dtype=F32),
            vmem(4, 2, 24, 128),
            vmem(8, 2, 24, 128),
            vmem(8, 24, 128),
            vmem(2, 4, 24, 128),
            vmem(8, 2, 24, 128, dtype=F32),
            vmem(2, 4, 24, 128, dtype=F32),
            vmem(32, 768, dtype=F32),
            vmem(64, 1152),
            vmem(6, 128, dtype=F32),
            pltpu.SMEM((12,), F32),
            vmem(8, 8, 128, dtype=F32),
            vmem(8, 8, 128, dtype=F32),
            vmem(8, 8, 128, dtype=F32),
            vmem(8, 8, 128, dtype=F32),
            vmem(4, 8, 128, dtype=F32),
            vmem(4, 8, 128, dtype=F32),
            vmem(8, 8, 128, dtype=F32),
            vmem(2, 8, 128, dtype=F32),
            dma(14),
            dma(23),
            dma(4),
            dma(4),
            one,
            dma(4),
            one,
            dma(2, 4, 4),
            dma(36),
            one,
            dma(9),
            dma(9),
            dma(36),
            dma(36),
            one,
            one,
            one,
            one,
            one,
            one,
            one,
            one,
            one,
        ],
        compiler_params=pltpu.CompilerParams(
            collective_id=0, has_side_effects=True, vmem_limit_bytes=62 << 20
        ),
        name="axial_layer",
    )(
        tiles(skip_stream_input),
        tiles(lateral_asking_vectors),
        tiles(lateral_matched_vectors),
        tiles(lateral_carried_vectors),
        lateral_closing_linear,
        upright_normalizer_multiplier.reshape(6, 128),
        upright_threefold_linear.T,
        upright_closing_linear,
        regression_factors,
        regression_offset,
    )
    return aligned.transpose(0, 2, 1, 3).reshape(4, 8, 768), pairs


def solution(mesh):
    placed = (
        P("seq", "pos", None),
        P("seq", "pos", None),
        P("seq", "pos", None),
        P("seq", "pos", None),
        P(),
        P(),
        P(None, "seq"),
        P(),
        P(),
        P(),
    )
    return jax.shard_map(
        per_device,
        mesh=mesh,
        in_specs=placed,
        out_specs=(P("seq", "pos", None), P("pos", "seq")),
        check_vma=False,
    )
```
